1024 devices in a mesh: coarse: 16 (over y, x_hi), fine: 64 (over x_lo, z, core).
Axes of the slice: x: 4 (x_hi: 2, x_lo: 2; x = x_hi * 2 + x_lo), y: 8, z: 16, core: 2. Of those that a mesh axis runs over, the one named last changes fastest.
Arguments:
- embeddings: bfloat16 [524288, 512], P(('coarse', 'fine')), may hold values from -64 to 64
- labels: int32 [524288, 1], P(('coarse', 'fine')), may hold values from 0 to 63; in each aligned block of 512 rows (0 to 511, 512 to 1023, ...) at most 16 rows name the same one
Outputs:
- max_similarity: float32 [524288], P(('coarse', 'fine'))
The draws below stay inside these ranges and needn't reach their ends.
Inputs may be any that keep to these rules, and one draw needn't show every extreme that they name: `labels`: among the rows of one device no label appears more than 16 times; on some device one label appears exactly 16 times.
All inputs are finite; a program needn't handle non-finite values. Where the reference program divides by a largest or mean magnitude, that divisor is 1e-20 or more.
Results may differ from the reference program's by a relative error of at most 0.00035.
The reference program's roundings to bfloat16 on the way count: a program that leaves them out, or rounds other values in their place, can miss the bound.
Values may be sent and summed in bfloat16 or wider, within the bound.
No kernel may reach another device: no remote copies, remote signals or barrier semaphores. Data moves between devices by JAX's collectives and lax.ppermute only.
A program may use at most 32 MiB of HBM per device.

```python
import math
import jax
import jax.numpy as jnp
import numpy as np
from jax import lax

D = 512
ROW_DEV = 512
ITERS = 2
ROWS = 524288
GROUP_ROWS = 32768
CAP = 16
N_COARSE = 16
N_FINE = 64


def draw_embeddings(key, part):
    keys = jax.random.split(key, 7)
    row_pos = (jnp.arange(ROWS, dtype=jnp.float32) / ROWS)[:, None]
    column_phase = jax.random.uniform(keys[0], (D,), jnp.float32, 0.0, 2.0 * math.pi)
    column_scale = jnp.exp(0.8 * jnp.cos(column_phase[None, :] + math.pi * row_pos))
    first_mean = jnp.clip(jax.random.normal(keys[1], (D,), jnp.float32), -3.0, 3.0)
    second_mean = jnp.clip(jax.random.normal(keys[2], (D,), jnp.float32), -3.0, 3.0)
    noise = jnp.clip(jax.random.normal(keys[3], (ROWS, D), jnp.float32), -4.0, 4.0)
    row_scale = jnp.exp(jax.random.uniform(keys[4], (ROWS, 1), jnp.float32, 0.0, math.log(10.0)))
    strength = 0.7
    heavy_device = jax.random.randint(keys[5], (), 0, ROWS // ROW_DEV)
    row_device = (jnp.arange(ROWS, dtype=jnp.int32) // ROW_DEV)[:, None]
    on_heavy = (row_device == heavy_device).astype(jnp.float32)
    boosted = (jax.random.randint(keys[6], (1, D), 0, 4) == 0).astype(jnp.float32)
    row_scale = row_scale * (1.0 - on_heavy) + 4.0 * on_heavy
    column_boost = 1.0 + 4.0 * on_heavy * boosted
    mixed = column_scale * column_boost * noise
    mixed = mixed + 0.6 * jnp.roll(mixed, 1, axis=1)
    common = strength * (first_mean[None, :] * jnp.cos(math.pi * row_pos) + second_mean[None, :] * jnp.sin(math.pi * row_pos))
    values = jnp.clip(row_scale * (mixed + common), -64.0, 64.0)
    return values.astype(jnp.bfloat16)


def shared_out(key, own, number, rows, amount, top, limit, slope):
    order = jax.random.permutation(key, amount)
    heavy_load, usual = load_shares(amount, rows * top, limit, slope, True), load_shares(amount, rows * top, limit, slope, False)
    places = jnp.arange(amount)

    def named(lengths, turn):
        used = int((lengths > 0).sum())
        fixed = max(1, used // 4)
        passed = fixed + (places - fixed + turn * (used - fixed)) % max(1, amount - fixed)
        return jnp.zeros((amount,), jnp.int32).at[order[jnp.where(places < fixed, places, passed)]].set(jnp.asarray(lengths, jnp.int32))

    lengths = jnp.where(number % 4 == 0, named(heavy_load, number // 4), named(usual, number - number // 4 - 1))
    mixed = jax.random.permutation(jax.random.fold_in(own, 3), amount)
    source_of, receiver = mixed[0:amount // 2 * 2:2], mixed[1:amount // 2 * 2:2]
    margin = jnp.minimum(lengths[source_of] - 1, limit - lengths[receiver]) // 2
    margin = jnp.where((source_of == order[0]) | (receiver == order[0]) | (lengths[receiver] == 0), 0, jnp.maximum(margin, 0))
    passed = jax.random.randint(jax.random.fold_in(own, 4), (amount // 2,), 0, 1 << 20) % (margin + 1)
    lengths = lengths.at[source_of].add(-passed).at[receiver].add(passed)
    items = jnp.searchsorted(jnp.cumsum(lengths), jnp.arange(rows * top), side="right").astype(jnp.int32)
    table = items.reshape(top, rows).T
    table = table[jax.random.permutation(jax.random.fold_in(own, 1), rows)]
    turn = jax.random.randint(jax.random.fold_in(own, 2), (rows, 1), 0, top)
    return jnp.take_along_axis(table, (jnp.arange(top)[None, :] + turn) % top, axis=1)


def load_shares(number_of, total, most, slope, full):
    portions = [(1 << 20) // math.isqrt(rank ** slope) + 1 for rank in range(1, number_of + 1)]
    largest = most if full else min(most, max(-(-total // number_of), total * portions[0] // sum(portions)))
    least = 1 if total - largest >= number_of - 1 else 0
    given, surplus = [largest] + [least] * (number_of - 1), total - largest - least * (number_of - 1)
    while surplus > 0:
        candidates = [i for i in range(1, number_of) if given[i] < largest] or [i for i in range(1, number_of) if given[i] < most]
        mass, left = sum([portions[i] for i in candidates]), surplus
        for i in candidates:
            addition = min(most - given[i], max(1, left * portions[i] // mass), surplus)
            given[i] = given[i] + addition
            surplus = surplus - addition
    return np.array(given)


def setup_inputs(seed: int = 0) -> dict:
    splits = jax.random.split(jax.random.key(seed), 3)
    embeddings = draw_embeddings(jax.random.fold_in(splits[2], 71), 0)
    labels_keys = jax.random.split(jax.random.fold_in(splits[1], 1), ROWS // ROW_DEV)
    labels_turns = jax.random.permutation(jax.random.fold_in(splits[1], 3), ROWS // ROW_DEV)
    labels = jax.vmap(lambda own, number: shared_out(jax.random.fold_in(splits[1], 2), own, number, ROW_DEV, N_FINE, 1, CAP, 2))(labels_keys, labels_turns).reshape((ROWS, 1))
    return dict(embeddings=embeddings, labels=labels)


EPS = 1e-06
RIDGE = 0.001

def matmul_high(left, right):
    return jnp.dot(left, right, precision=lax.Precision.HIGHEST, preferred_element_type=jnp.float32)

def inverse_root(second):
    identity = jnp.eye(second.shape[0], dtype=jnp.float32)
    norm_scale = jnp.max(lax.optimization_barrier(jnp.sum(jnp.abs(second), axis=1)))
    root_est = second / norm_scale
    inverse_est = identity
    for sweep in range(ITERS):
        newton_step = 0.5 * (3.0 * identity - matmul_high(inverse_est, root_est))
        root_est = matmul_high(root_est, newton_step)
        inverse_est = matmul_high(newton_step, inverse_est)
    return (inverse_est / jnp.sqrt(norm_scale)).astype(jnp.bfloat16)

def unit_rows(values, whiten_b):
    whitened = jnp.dot(values, whiten_b, preferred_element_type=jnp.float32)
    width_value = whitened.shape[-1]
    meansq = lax.optimization_barrier(jnp.mean(whitened * whitened, axis=-1, keepdims=True))
    return (whitened * lax.rsqrt(width_value * (meansq + EPS))).astype(jnp.bfloat16)

def label_best(pieces):
    buffer_rows, valid_slots = pieces
    similar = jnp.dot(buffer_rows, buffer_rows.T, preferred_element_type=jnp.float32)
    slot_total = buffer_rows.shape[0]
    keep_mask = (valid_slots[None, :] > 0) & jnp.logical_not(jnp.eye(slot_total, dtype=bool))
    return lax.optimization_barrier(jnp.max(jnp.where(keep_mask, similar, -1.0), axis=1))

def reference(embeddings, labels):
    second = lax.dot_general(embeddings, embeddings, (((0,), (0,)), ((), ())), preferred_element_type=jnp.float32)
    second = second / ROWS + RIDGE * jnp.eye(D, dtype=jnp.float32)
    whiten_b = inverse_root(second)
    grouped = embeddings.reshape(N_COARSE, GROUP_ROWS, D)
    group_labels = labels.reshape(N_COARSE, N_FINE, ROW_DEV)

    def group_best(pieces):
        group_rows, owner_label = pieces
        unit_values = unit_rows(group_rows, whiten_b)
        onehot = (owner_label[..., None] == jnp.arange(N_FINE, dtype=jnp.int32)).astype(jnp.int32)
        rank_before = jnp.cumsum(onehot, axis=1, dtype=jnp.int32) - onehot
        slot_index = lax.optimization_barrier(jnp.sum(rank_before * onehot, axis=2)).astype(jnp.int32)
        source = jnp.arange(N_FINE, dtype=jnp.int32)[:, None]
        position = (source * CAP + slot_index).reshape(-1).astype(jnp.int32)
        flat_label = owner_label.reshape(-1).astype(jnp.int32)
        buffers = jnp.zeros((N_FINE, N_FINE * CAP, D), jnp.bfloat16).at[flat_label, position].set(unit_values)
        valid_slots = jnp.zeros((N_FINE, N_FINE * CAP), jnp.float32).at[flat_label, position].set(1.0)
        best_match = lax.map(label_best, (buffers, valid_slots))
        return best_match[flat_label, position]
    return lax.map(group_best, (grouped, group_labels)).reshape(ROWS)
```

```python
import functools

import jax
import jax.numpy as jnp
from jax import lax
from jax.experimental import pallas as pl
from jax.experimental.pallas import tpu as pltpu
from jax.sharding import Mesh, PartitionSpec as P

ITERS = 2
EPS = 1e-06
RIDGE = 0.001

AXES = ("y", "xh", "xl", "z", "c")
SIZES = (8, 2, 2, 16, 2)
FINE = ("xl", "z", "c")
PLANE = ("y", "xh", "xl", "c")

D = 512
ROW_DEV = 512
ROWS = 524288
N_FINE = 64
N_PLANE = 64
N_Z = 16
CAP = 16
SLOTS = N_FINE * CAP
BLOCK = 128
BLOCKS = D // BLOCK
STRIP = 3 * BLOCK
STRIP_ROWS = D // N_PLANE

F32 = jnp.float32
BF16 = jnp.bfloat16


def iota(shape, dim):
    return lax.broadcasted_iota(jnp.int32, shape, dim)


def call(body, outs, flops, moved, scratch=(), name=None):
    return pl.pallas_call(
        body,
        out_shape=outs,
        scratch_shapes=scratch,
        name=name,
        compiler_params=pltpu.CompilerParams(vmem_limit_bytes=48 << 20),
        cost_estimate=pl.CostEstimate(flops=flops, bytes_accessed=moved, transcendentals=0),
    )


def gram_body(rows_ref, out_ref):
    rows = rows_ref[...]
    gram = lax.dot_general(rows, rows, (((0,), (0,)), ((), ())), preferred_element_type=F32)
    for b in range(BLOCKS):
        for k in range(3):
            c = (b + k) % BLOCKS
            out_ref[b * BLOCK:(b + 1) * BLOCK, k * BLOCK:(k + 1) * BLOCK] = gram[
                b * BLOCK:(b + 1) * BLOCK, c * BLOCK:(c + 1) * BLOCK
            ].astype(out_ref.dtype)


def pack_body(label_ref, rows_ref, out_ref, slot_ref):
    label = label_ref[...]
    onehot = (iota((N_FINE, ROW_DEV), 0) == label).astype(F32)
    earlier = (iota((ROW_DEV, ROW_DEV), 0) < iota((ROW_DEV, ROW_DEV), 1)).astype(BF16)
    rank = jnp.dot(onehot.astype(BF16), earlier, preferred_element_type=F32)
    slot = jnp.sum(onehot * rank, axis=0, keepdims=True).astype(jnp.int32)
    slot_ref[...] = slot
    place = label * CAP + slot
    chosen = (iota((SLOTS, ROW_DEV), 0) == place).astype(F32).astype(BF16)
    packed = jnp.dot(chosen, rows_ref[...], preferred_element_type=F32)
    filled = jnp.dot(chosen, jnp.ones((ROW_DEV, BLOCK), BF16), preferred_element_type=F32) > 0.5
    for k in range(D // BLOCK):
        part = packed[:, k * BLOCK:(k + 1) * BLOCK]
        out_ref[:, k * BLOCK:(k + 1) * BLOCK] = jnp.where(filled, part, jnp.nan).astype(BF16)


def high(left, right):
    return jnp.dot(left, right, precision=lax.Precision.HIGHEST, preferred_element_type=F32)


def root_body(strip_ref, out_ref, full_ref):
    for b in range(BLOCKS):
        for k in range(BLOCKS):
            c = (b + k) % BLOCKS
            if k < 3:
                piece = strip_ref[b * BLOCK:(b + 1) * BLOCK, k * BLOCK:(k + 1) * BLOCK]
            else:
                piece = strip_ref[c * BLOCK:(c + 1) * BLOCK, BLOCK:2 * BLOCK].T
            full_ref[b * BLOCK:(b + 1) * BLOCK, c * BLOCK:(c + 1) * BLOCK] = piece
    identity = (iota((D, D), 0) == iota((D, D), 1)).astype(F32)
    second = full_ref[...] / ROWS + RIDGE * identity
    norm_scale = jnp.max(jnp.sum(jnp.abs(second), axis=0, keepdims=True), axis=1, keepdims=True)
    root_est = second / norm_scale
    inverse_est = 0.5 * (3.0 * identity - root_est)
    root_est = high(root_est, inverse_est)
    newton_step = 0.5 * (3.0 * identity - high(inverse_est, root_est))
    inverse_est = high(newton_step, inverse_est)
    out_ref[...] = (inverse_est / jnp.sqrt(norm_scale)).astype(BF16)


def best_body(rows_ref, whiten_ref, out_ref):
    rows = rows_ref[...].astype(F32)
    present = rows == rows
    clean = jnp.where(present, rows, 0.0).astype(BF16)
    whitened = jnp.dot(clean, whiten_ref[...], preferred_element_type=F32)
    meansq = jnp.mean(whitened * whitened, axis=-1, keepdims=True)
    unit = (whitened * lax.rsqrt(D * (meansq + EPS))).astype(BF16)
    bias = jnp.where(present[:, :1], 0.0, -4.0)
    tile = 256
    best = jnp.full((1, SLOTS), -1.0, F32)
    for b in range(SLOTS // tile):
        lo = b * tile
        similar = lax.dot_general(
            unit[lo:lo + tile], unit, (((1,), (1,)), ((), ())), preferred_element_type=F32
        )
        similar = similar + bias[lo:lo + tile]
        similar = jnp.where(
            iota((tile, SLOTS), 0) + lo == iota((tile, SLOTS), 1), -1.0, similar
        )
        best = jnp.maximum(best, jnp.max(similar, axis=0, keepdims=True))
    spread = jnp.where(iota((N_FINE, SLOTS), 1) // CAP == iota((N_FINE, SLOTS), 0), best, 0.0)
    fold = (iota((SLOTS, CAP), 0) % CAP == iota((SLOTS, CAP), 1)).astype(F32)
    out_ref[...] = high(spread, fold)


def pick_body(label_ref, slot_ref, best_ref, out_ref):
    onehot = (iota((N_FINE, ROW_DEV), 0) == label_ref[...]).astype(F32)
    mine = lax.dot_general(
        best_ref[...], onehot, (((0,), (0,)), ((), ())),
        precision=lax.Precision.HIGHEST, preferred_element_type=F32,
    )
    chosen = iota((CAP, ROW_DEV), 0) == slot_ref[...]
    out_ref[...] = jnp.sum(jnp.where(chosen, mine, 0.0), axis=0, keepdims=True)


def swap(value, axes):
    return lax.all_to_all(value, axes, split_axis=0, concat_axis=0, tiled=True)


def per_device(embeddings, labels):
    label = labels.reshape(1, ROW_DEV)
    strips = call(
        gram_body, jax.ShapeDtypeStruct((D, STRIP), BF16), 2 * ROW_DEV * D * D, 1 << 20, name="gram"
    )(embeddings)
    parts = swap(strips.reshape(N_PLANE, STRIP_ROWS, STRIP), PLANE)

    outgoing, slot = call(
        pack_body,
        (
            jax.ShapeDtypeStruct((SLOTS, D), BF16),
            jax.ShapeDtypeStruct((1, ROW_DEV), jnp.int32),
        ),
        2 * SLOTS * ROW_DEV * D, 2 << 20, name="pack",
    )(label, embeddings)
    received = swap(outgoing.reshape(N_FINE, CAP, D), FINE).reshape(SLOTS, D)

    strip = jnp.sum(parts.astype(F32), axis=0)
    layers = swap(jnp.broadcast_to(strip, (N_Z, STRIP_ROWS, STRIP)), "z")
    strip = jnp.sum(layers, axis=0)
    whole = swap(jnp.broadcast_to(strip, (N_PLANE, STRIP_ROWS, STRIP)), PLANE).reshape(D, STRIP)
    whiten_b = call(
        root_body, jax.ShapeDtypeStruct((D, D), BF16), 36 * D * D * D, 2 << 20,
        (pltpu.VMEM((D, D), F32),), name="root",
    )(whole)

    best = call(
        best_body, jax.ShapeDtypeStruct((N_FINE, CAP), F32),
        2 * SLOTS * D * (D + SLOTS), 2 << 20, name="best",
    )(received, whiten_b)
    returned = swap(best.reshape(N_FINE, 1, CAP), FINE).reshape(N_FINE, CAP)
    picked = call(
        pick_body, jax.ShapeDtypeStruct((1, ROW_DEV), F32), 1 << 20, 1 << 16, name="pick"
    )(label, slot, returned)
    return picked.reshape(ROW_DEV)


def solution(mesh):
    fine = Mesh(mesh.devices.reshape(SIZES), AXES)
    return jax.shard_map(
        per_device,
        mesh=fine,
        in_specs=(P(AXES, None), P(AXES, None)),
        out_specs=P(AXES),
        check_vma=False,
    )
```

```python
import functools

import jax
import jax.numpy as jnp
from jax import lax
from jax.experimental import pallas as pl
from jax.experimental.pallas import tpu as pltpu
from jax.sharding import Mesh, PartitionSpec as P

ITERS = 2
EPS = 1e-06
RIDGE = 0.001

AXES = ("y", "xh", "xl", "z", "c")
SIZES = (8, 2, 2, 16, 2)
FINE = ("xl", "z", "c")
PLANE = ("y", "xh", "xl", "c")

D = 512
ROW_DEV = 512
ROWS = 524288
N_FINE = 64
N_PLANE = 64
N_Z = 16
CAP = 16
SLOTS = N_FINE * CAP
BLOCK = 128
BLOCKS = D // BLOCK
STRIP = 3 * BLOCK
STRIP_ROWS = D // N_PLANE
FIRST = (8, 7, 9, 1, 15, 2, 14)
SECOND = (6, 10, 5, 11, 4, 12, 3, 13)

F32 = jnp.float32
BF16 = jnp.bfloat16


def iota(shape, dim):
    return lax.broadcasted_iota(jnp.int32, shape, dim)


VMEM = pl.BlockSpec(memory_space=pltpu.VMEM)
SMEM = pl.BlockSpec(memory_space=pltpu.SMEM)


def call(body, outs, flops, moved, scratch=(), name=None, specs=None):
    return pl.pallas_call(
        body,
        **({} if specs is None else dict(in_specs=specs)),
        out_shape=outs,
        scratch_shapes=scratch,
        name=name,
        compiler_params=pltpu.CompilerParams(vmem_limit_bytes=48 << 20),
        cost_estimate=pl.CostEstimate(flops=flops, bytes_accessed=moved, transcendentals=0),
    )


def gram_body(rows_ref, out_ref):
    rows = rows_ref[...]
    gram = lax.dot_general(rows, rows, (((0,), (0,)), ((), ())), preferred_element_type=F32)
    for b in range(BLOCKS):
        for k in range(3):
            c = (b + k) % BLOCKS
            out_ref[b * BLOCK:(b + 1) * BLOCK, k * BLOCK:(k + 1) * BLOCK] = gram[
                b * BLOCK:(b + 1) * BLOCK, c * BLOCK:(c + 1) * BLOCK
            ].astype(out_ref.dtype)


def split(index):
    return index // (2 * N_Z), (index // 2) % N_Z, index % 2


def pack_body(me_ref, label_ref, rows_ref, *refs):
    outs, slot_ref = refs[:4], refs[4]
    label = label_ref[...]
    onehot = (iota((N_FINE, ROW_DEV), 0) == label).astype(F32)
    earlier = (iota((ROW_DEV, ROW_DEV), 0) < iota((ROW_DEV, ROW_DEV), 1)).astype(BF16)
    rank = jnp.dot(onehot.astype(BF16), earlier, preferred_element_type=F32)
    slot = jnp.sum(onehot * rank, axis=0, keepdims=True).astype(jnp.int32)
    slot_ref[...] = slot
    xl, z, c = split(me_ref[0])
    to_xl, to_z, to_c = split(label)
    block = (to_xl ^ xl) * 2 + (to_c ^ c)
    place = (block * N_Z + ((to_z - z + N_Z) % N_Z)) * CAP + slot
    chosen = (iota((SLOTS, ROW_DEV), 0) == place).astype(F32).astype(BF16)
    packed = jnp.dot(chosen, rows_ref[...], preferred_element_type=F32)
    filled = jnp.dot(chosen, jnp.ones((ROW_DEV, BLOCK), BF16), preferred_element_type=F32) > 0.5
    for k in range(D // BLOCK):
        part = packed[:, k * BLOCK:(k + 1) * BLOCK]
        part = jnp.where(filled, part, jnp.nan).astype(BF16)
        for e in range(4):
            outs[e][:, k * BLOCK:(k + 1) * BLOCK] = part[e * N_Z * CAP:(e + 1) * N_Z * CAP]


def turn_body(*refs):
    for d in range(N_Z):
        for e in range(4):
            refs[4 + d][e * CAP:(e + 1) * CAP, :] = refs[e][d * CAP:(d + 1) * CAP, :]


def high(left, right):
    return jnp.dot(left, right, precision=lax.Precision.HIGHEST, preferred_element_type=F32)


def root_body(strip_ref, out_ref, full_ref):
    for b in range(BLOCKS):
        for k in range(BLOCKS):
            c = (b + k) % BLOCKS
            if k < 3:
                piece = strip_ref[b * BLOCK:(b + 1) * BLOCK, k * BLOCK:(k + 1) * BLOCK]
            else:
                piece = strip_ref[c * BLOCK:(c + 1) * BLOCK, BLOCK:2 * BLOCK].T
            full_ref[b * BLOCK:(b + 1) * BLOCK, c * BLOCK:(c + 1) * BLOCK] = piece
    identity = (iota((D, D), 0) == iota((D, D), 1)).astype(F32)
    second = full_ref[...] / ROWS + RIDGE * identity
    norm_scale = jnp.max(jnp.sum(jnp.abs(second), axis=0, keepdims=True), axis=1, keepdims=True)
    root_est = second / norm_scale
    inverse_est = 0.5 * (3.0 * identity - root_est)
    root_est = high(root_est, inverse_est)
    newton_step = 0.5 * (3.0 * identity - high(inverse_est, root_est))
    inverse_est = high(newton_step, inverse_est)
    out_ref[...] = (inverse_est / jnp.sqrt(norm_scale)).astype(BF16)


def best_body(me_ref, whiten_ref, *refs):
    out_ref = refs[N_Z]
    rows = jnp.concatenate([ref[...] for ref in refs[:N_Z]], axis=0).astype(F32)
    present = rows == rows
    clean = jnp.where(present, rows, 0.0).astype(BF16)
    whitened = jnp.dot(clean, whiten_ref[...], preferred_element_type=F32)
    meansq = jnp.mean(whitened * whitened, axis=-1, keepdims=True)
    unit = (whitened * lax.rsqrt(D * (meansq + EPS))).astype(BF16)
    bias = jnp.where(present[:, :1], 0.0, -4.0)
    tile = 256
    best = jnp.full((1, SLOTS), -1.0, F32)
    for b in range(SLOTS // tile):
        lo = b * tile
        similar = lax.dot_general(
            unit[lo:lo + tile], unit, (((1,), (1,)), ((), ())), preferred_element_type=F32
        )
        similar = similar + bias[lo:lo + tile]
        similar = jnp.where(
            iota((tile, SLOTS), 0) + lo == iota((tile, SLOTS), 1), -1.0, similar
        )
        best = jnp.maximum(best, jnp.max(similar, axis=0, keepdims=True))
    xl, z, c = split(me_ref[0])
    column = iota((1, SLOTS), 1) // CAP
    block, step = column % 4, column // 4
    source = ((xl ^ (block // 2)) * N_Z + ((z - step + N_Z) % N_Z)) * 2 + (c ^ (block % 2))
    spread = jnp.where(source == iota((N_FINE, SLOTS), 0), best, 0.0)
    fold = (iota((SLOTS, CAP), 0) % CAP == iota((SLOTS, CAP), 1)).astype(F32)
    out_ref[...] = high(spread, fold)


def pick_body(label_ref, slot_ref, best_ref, out_ref):
    onehot = (iota((N_FINE, ROW_DEV), 0) == label_ref[...]).astype(F32)
    mine = lax.dot_general(
        best_ref[...], onehot, (((0,), (0,)), ((), ())),
        precision=lax.Precision.HIGHEST, preferred_element_type=F32,
    )
    chosen = iota((CAP, ROW_DEV), 0) == slot_ref[...]
    out_ref[...] = jnp.sum(jnp.where(chosen, mine, 0.0), axis=0, keepdims=True)


def swap(value, axes):
    return lax.all_to_all(value, axes, split_axis=0, concat_axis=0, tiled=True)


def per_device(embeddings, labels):
    label = labels.reshape(1, ROW_DEV)
    strips = call(
        gram_body, jax.ShapeDtypeStruct((D, STRIP), BF16), 2 * ROW_DEV * D * D, 1 << 20, name="gram"
    )(embeddings)
    parts = swap(strips.reshape(N_PLANE, STRIP_ROWS, STRIP), PLANE)

    me = lax.axis_index(FINE).reshape(1)
    *blocks, slot = call(
        pack_body,
        (jax.ShapeDtypeStruct((N_Z * CAP, D), BF16),) * 4
        + (jax.ShapeDtypeStruct((1, ROW_DEV), jnp.int32),),
        2 * SLOTS * ROW_DEV * D, 2 << 20, name="pack", specs=(SMEM, VMEM, VMEM),
    )(me, label, embeddings)
    blocks = [
        block if e == 0 else lax.ppermute(block, ("xl", "c"), [(i, i ^ e) for i in range(4)])
        for e, block in enumerate(blocks)
    ]
    parts, *blocks = lax.optimization_barrier((parts, *blocks))
    received = list(call(
        turn_body, (jax.ShapeDtypeStruct((4 * CAP, D), BF16),) * N_Z, 0, 2 << 20, name="turn"
    )(*blocks))

    def send(steps):
        for d in steps:
            received[d] = lax.ppermute(received[d], "z", [(i, (i + d) % N_Z) for i in range(N_Z)])

    strip = jnp.sum(parts.astype(F32), axis=0)
    layers = swap(jnp.broadcast_to(strip, (N_Z, STRIP_ROWS, STRIP)), "z")
    send(FIRST)
    layers, *received = lax.optimization_barrier((layers, *received))
    strip = jnp.sum(layers, axis=0)
    whole = swap(jnp.broadcast_to(strip, (N_PLANE, STRIP_ROWS, STRIP)), PLANE)
    send(SECOND)
    whole, *received = lax.optimization_barrier((whole, *received))
    whole = whole.reshape(D, STRIP)
    whiten_b = call(
        root_body, jax.ShapeDtypeStruct((D, D), BF16), 36 * D * D * D, 2 << 20,
        (pltpu.VMEM((D, D), F32),), name="root",
    )(whole)

    best = call(
        best_body, jax.ShapeDtypeStruct((N_FINE, CAP), F32),
        2 * SLOTS * D * (D + SLOTS), 2 << 20, name="best",
        specs=(SMEM,) + (VMEM,) * (N_Z + 1),
    )(me, whiten_b, *received)
    returned = swap(best.reshape(N_FINE, 1, CAP), FINE).reshape(N_FINE, CAP)
    picked = call(
        pick_body, jax.ShapeDtypeStruct((1, ROW_DEV), F32), 1 << 20, 1 << 16, name="pick"
    )(label, slot, returned)
    return picked.reshape(ROW_DEV)


def solution(mesh):
    fine = Mesh(mesh.devices.reshape(SIZES), AXES)
    return jax.shard_map(
        per_device,
        mesh=fine,
        in_specs=(P(AXES, None), P(AXES, None)),
        out_specs=P(AXES),
        check_vma=False,
    )
```

```python
import functools

import jax
import jax.numpy as jnp
from jax import lax
from jax.experimental import pallas as pl
from jax.experimental.pallas import tpu as pltpu
from jax.sharding import Mesh, PartitionSpec as P

ITERS = 2
EPS = 1e-06
RIDGE = 0.001

AXES = ("y", "xh", "xl", "z", "c")
SIZES = (8, 2, 2, 16, 2)
FINE = ("xl", "z", "c")
PLANE = ("y", "xh", "xl", "c")

D = 512
ROW_DEV = 512
ROWS = 524288
N_FINE = 64
N_PLANE = 64
N_Z = 16
CAP = 16
SLOTS = N_FINE * CAP
BLOCK = 128
BLOCKS = D // BLOCK
STRIP = 3 * BLOCK
STRIP_ROWS = D // N_PLANE

F32 = jnp.float32
BF16 = jnp.bfloat16


def iota(shape, dim):
    return lax.broadcasted_iota(jnp.int32, shape, dim)


def call(body, outs, flops, moved, scratch=(), name=None):
    return pl.pallas_call(
        body,
        out_shape=outs,
        scratch_shapes=scratch,
        name=name,
        compiler_params=pltpu.CompilerParams(vmem_limit_bytes=48 << 20),
        cost_estimate=pl.CostEstimate(flops=flops, bytes_accessed=moved, transcendentals=0),
    )


def gram_body(rows_ref, out_ref):
    rows = rows_ref[...]
    gram = lax.dot_general(rows, rows, (((0,), (0,)), ((), ())), preferred_element_type=F32)
    for b in range(BLOCKS):
        for k in range(3):
            c = (b + k) % BLOCKS
            out_ref[b * BLOCK:(b + 1) * BLOCK, k * BLOCK:(k + 1) * BLOCK] = gram[
                b * BLOCK:(b + 1) * BLOCK, c * BLOCK:(c + 1) * BLOCK
            ].astype(out_ref.dtype)


def pack_body(label_ref, rows_ref, out_ref, slot_ref):
    label = label_ref[...]
    onehot = (iota((N_FINE, ROW_DEV), 0) == label).astype(F32)
    earlier = (iota((ROW_DEV, ROW_DEV), 0) < iota((ROW_DEV, ROW_DEV), 1)).astype(BF16)
    rank = jnp.dot(onehot.astype(BF16), earlier, preferred_element_type=F32)
    slot = jnp.sum(onehot * rank, axis=0, keepdims=True).astype(jnp.int32)
    slot_ref[...] = slot
    place = label * CAP + slot
    chosen = (iota((SLOTS, ROW_DEV), 0) == place).astype(F32).astype(BF16)
    packed = jnp.dot(chosen, rows_ref[...], preferred_element_type=F32)
    filled = jnp.dot(chosen, jnp.ones((ROW_DEV, BLOCK), BF16), preferred_element_type=F32) > 0.5
    for k in range(D // BLOCK):
        part = packed[:, k * BLOCK:(k + 1) * BLOCK]
        out_ref[:, k * BLOCK:(k + 1) * BLOCK] = jnp.where(filled, part, jnp.nan).astype(BF16)


def high(left, right):
    return jnp.dot(left, right, precision=lax.Precision.HIGHEST, preferred_element_type=F32)


def root_body(strip_ref, out_ref, full_ref):
    for b in range(BLOCKS):
        for k in range(BLOCKS):
            c = (b + k) % BLOCKS
            if k < 3:
                piece = strip_ref[b * BLOCK:(b + 1) * BLOCK, k * BLOCK:(k + 1) * BLOCK]
            else:
                piece = strip_ref[c * BLOCK:(c + 1) * BLOCK, BLOCK:2 * BLOCK].T
            full_ref[b * BLOCK:(b + 1) * BLOCK, c * BLOCK:(c + 1) * BLOCK] = piece
    identity = (iota((D, D), 0) == iota((D, D), 1)).astype(F32)
    second = full_ref[...] / ROWS + RIDGE * identity
    norm_scale = jnp.max(jnp.sum(jnp.abs(second), axis=0, keepdims=True), axis=1, keepdims=True)
    root_est = second / norm_scale
    inverse_est = 0.5 * (3.0 * identity - root_est)
    root_est = high(root_est, inverse_est)
    newton_step = 0.5 * (3.0 * identity - high(inverse_est, root_est))
    inverse_est = high(newton_step, inverse_est)
    out_ref[...] = (inverse_est / jnp.sqrt(norm_scale)).astype(BF16)


def best_body(rows_ref, whiten_ref, out_ref):
    rows = rows_ref[...].astype(F32)
    present = rows == rows
    clean = jnp.where(present, rows, 0.0).astype(BF16)
    whitened = jnp.dot(clean, whiten_ref[...], preferred_element_type=F32)
    meansq = jnp.mean(whitened * whitened, axis=-1, keepdims=True)
    unit = (whitened * lax.rsqrt(D * (meansq + EPS))).astype(BF16)
    bias = jnp.where(present[:, :1], 0.0, -4.0)
    tile = 256
    best = jnp.full((1, SLOTS), -1.0, F32)
    for b in range(SLOTS // tile):
        lo = b * tile
        similar = lax.dot_general(
            unit[lo:lo + tile], unit, (((1,), (1,)), ((), ())), preferred_element_type=F32
        )
        similar = similar + bias[lo:lo + tile]
        similar = jnp.where(
            iota((tile, SLOTS), 0) + lo == iota((tile, SLOTS), 1), -1.0, similar
        )
        best = jnp.maximum(best, jnp.max(similar, axis=0, keepdims=True))
    spread = jnp.where(iota((N_FINE, SLOTS), 1) // CAP == iota((N_FINE, SLOTS), 0), best, 0.0)
    fold = (iota((SLOTS, CAP), 0) % CAP == iota((SLOTS, CAP), 1)).astype(F32)
    out_ref[...] = high(spread, fold)


def pick_body(label_ref, slot_ref, best_ref, out_ref):
    onehot = (iota((N_FINE, ROW_DEV), 0) == label_ref[...]).astype(F32)
    mine = lax.dot_general(
        best_ref[...], onehot, (((0,), (0,)), ((), ())),
        precision=lax.Precision.HIGHEST, preferred_element_type=F32,
    )
    chosen = iota((CAP, ROW_DEV), 0) == slot_ref[...]
    out_ref[...] = jnp.sum(jnp.where(chosen, mine, 0.0), axis=0, keepdims=True)


def swap(value, axes):
    return lax.all_to_all(value, axes, split_axis=0, concat_axis=0, tiled=True)


def per_device(embeddings, labels):
    label = labels.reshape(1, ROW_DEV)
    strips = call(
        gram_body, jax.ShapeDtypeStruct((D, STRIP), BF16), 2 * ROW_DEV * D * D, 1 << 20, name="gram"
    )(embeddings)
    parts = swap(strips.reshape(N_PLANE, STRIP_ROWS, STRIP), PLANE)

    outgoing, slot = call(
        pack_body,
        (
            jax.ShapeDtypeStruct((SLOTS, D), BF16),
            jax.ShapeDtypeStruct((1, ROW_DEV), jnp.int32),
        ),
        2 * SLOTS * ROW_DEV * D, 2 << 20, name="pack",
    )(label, embeddings)
    received = swap(outgoing.reshape(N_FINE, CAP, D), FINE).reshape(SLOTS, D)

    strip = jnp.sum(parts.astype(F32), axis=0)
    for step in (1, 2, 4, 8):
        strip = strip + lax.ppermute(strip, "z", [(i, i ^ step) for i in range(N_Z)])
    strip, received = lax.optimization_barrier((strip, received))
    whole = swap(jnp.broadcast_to(strip, (N_PLANE, STRIP_ROWS, STRIP)), PLANE).reshape(D, STRIP)
    whiten_b = call(
        root_body, jax.ShapeDtypeStruct((D, D), BF16), 36 * D * D * D, 2 << 20,
        (pltpu.VMEM((D, D), F32),), name="root",
    )(whole)

    best = call(
        best_body, jax.ShapeDtypeStruct((N_FINE, CAP), F32),
        2 * SLOTS * D * (D + SLOTS), 2 << 20, name="best",
    )(received, whiten_b)
    returned = swap(best.reshape(N_FINE, 1, CAP), FINE).reshape(N_FINE, CAP)
    picked = call(
        pick_body, jax.ShapeDtypeStruct((1, ROW_DEV), F32), 1 << 20, 1 << 16, name="pick"
    )(label, slot, returned)
    return picked.reshape(ROW_DEV)


def solution(mesh):
    fine = Mesh(mesh.devices.reshape(SIZES), AXES)
    return jax.shard_map(
        per_device,
        mesh=fine,
        in_specs=(P(AXES, None), P(AXES, None)),
        out_specs=P(AXES),
        check_vma=False,
    )
```

```python
import math

import jax
import jax.numpy as jnp
from jax import lax
from jax.experimental import pallas as pl
from jax.experimental.pallas import tpu as pltpu
from jax.sharding import Mesh, PartitionSpec as P

ITERS = 2
EPS = 1e-06
RIDGE = 0.001

AXES = ("y", "xh", "xl", "z", "c")
SIZES = (8, 2, 2, 16, 2)
FINE = ("xl", "z", "c")
PLANE = ("y", "xh", "xl", "c")

D = 512
ROW_DEV = 512
ROWS = 524288
N_FINE = 64
N_PLANE = 64
N_Z = 16
CAP = 16
SLOTS = N_FINE * CAP
BLOCK = 128
BLOCKS = D // BLOCK
STRIP = 3 * BLOCK
STRIP_ROWS = D // N_PLANE
DOUBLING = (
    (("y",), 1, 8),
    (("y",), 2, 16),
    (("y",), 4, 32),
    (("xh", "xl"), 3, 6),
    (("xl",), 1, 2),
    (("c",), 1, 1),
)

F32 = jnp.float32
BF16 = jnp.bfloat16


def iota(shape, dim):
    return lax.broadcasted_iota(jnp.int32, shape, dim)


VMEM = pl.BlockSpec(memory_space=pltpu.VMEM)
SMEM = pl.BlockSpec(memory_space=pltpu.SMEM)


def call(body, outs, flops, moved, scratch=(), name=None, specs=None):
    return pl.pallas_call(
        body,
        **({} if specs is None else dict(in_specs=specs)),
        out_shape=outs,
        scratch_shapes=scratch,
        name=name,
        compiler_params=pltpu.CompilerParams(vmem_limit_bytes=48 << 20),
        cost_estimate=pl.CostEstimate(flops=flops, bytes_accessed=moved, transcendentals=0),
    )


def gram_body(rows_ref, out_ref):
    rows = rows_ref[...]
    gram = lax.dot_general(rows, rows, (((0,), (0,)), ((), ())), preferred_element_type=F32)
    for b in range(BLOCKS):
        for k in range(3):
            c = (b + k) % BLOCKS
            out_ref[b * BLOCK:(b + 1) * BLOCK, k * BLOCK:(k + 1) * BLOCK] = gram[
                b * BLOCK:(b + 1) * BLOCK, c * BLOCK:(c + 1) * BLOCK
            ].astype(out_ref.dtype)


def pack_body(label_ref, rows_ref, out_ref, slot_ref):
    label = label_ref[...]
    onehot = (iota((N_FINE, ROW_DEV), 0) == label).astype(F32)
    earlier = (iota((ROW_DEV, ROW_DEV), 0) < iota((ROW_DEV, ROW_DEV), 1)).astype(BF16)
    rank = jnp.dot(onehot.astype(BF16), earlier, preferred_element_type=F32)
    slot = jnp.sum(onehot * rank, axis=0, keepdims=True).astype(jnp.int32)
    slot_ref[...] = slot
    place = label * CAP + slot
    chosen = (iota((SLOTS, ROW_DEV), 0) == place).astype(F32).astype(BF16)
    packed = jnp.dot(chosen, rows_ref[...], preferred_element_type=F32)
    filled = jnp.dot(chosen, jnp.ones((ROW_DEV, BLOCK), BF16), preferred_element_type=F32) > 0.5
    for k in range(D // BLOCK):
        part = packed[:, k * BLOCK:(k + 1) * BLOCK]
        out_ref[:, k * BLOCK:(k + 1) * BLOCK] = jnp.where(filled, part, jnp.nan).astype(BF16)


def high(left, right):
    return jnp.dot(left, right, precision=lax.Precision.HIGHEST, preferred_element_type=F32)


def root_body(me_ref, near_ref, far_ref, out_ref, strip_ref, full_ref):
    half = N_PLANE // 2
    for k in range(N_PLANE):
        differs = 0
        for bit, (_, _, mask) in enumerate(DOUBLING):
            if k >> bit & 1:
                differs ^= mask
        source, at = (near_ref, k) if k < half else (far_ref, k - half)
        to = pl.multiple_of((me_ref[0] ^ differs) * STRIP_ROWS, STRIP_ROWS)
        strip_ref[pl.ds(to, STRIP_ROWS), :] = source[at * STRIP_ROWS:(at + 1) * STRIP_ROWS, :]
    for b in range(BLOCKS):
        for k in range(BLOCKS):
            c = (b + k) % BLOCKS
            if k < 3:
                piece = strip_ref[b * BLOCK:(b + 1) * BLOCK, k * BLOCK:(k + 1) * BLOCK]
            else:
                piece = strip_ref[c * BLOCK:(c + 1) * BLOCK, BLOCK:2 * BLOCK].T
            full_ref[b * BLOCK:(b + 1) * BLOCK, c * BLOCK:(c + 1) * BLOCK] = piece
    identity = (iota((D, D), 0) == iota((D, D), 1)).astype(F32)
    second = full_ref[...] / ROWS + RIDGE * identity
    norm_scale = jnp.max(jnp.sum(jnp.abs(second), axis=0, keepdims=True), axis=1, keepdims=True)
    root_est = second / norm_scale
    inverse_est = 0.5 * (3.0 * identity - root_est)
    root_est = high(root_est, inverse_est)
    newton_step = 0.5 * (3.0 * identity - high(inverse_est, root_est))
    inverse_est = high(newton_step, inverse_est)
    out_ref[...] = (inverse_est / jnp.sqrt(norm_scale)).astype(BF16)


def best_body(rows_ref, whiten_ref, out_ref):
    rows = rows_ref[...].astype(F32)
    present = rows == rows
    clean = jnp.where(present, rows, 0.0).astype(BF16)
    whitened = jnp.dot(clean, whiten_ref[...], preferred_element_type=F32)
    meansq = jnp.mean(whitened * whitened, axis=-1, keepdims=True)
    unit = (whitened * lax.rsqrt(D * (meansq + EPS))).astype(BF16)
    bias = jnp.where(present[:, :1], 0.0, -4.0)
    tile = 256
    best = jnp.full((1, SLOTS), -1.0, F32)
    for b in range(SLOTS // tile):
        lo = b * tile
        similar = lax.dot_general(
            unit[lo:lo + tile], unit, (((1,), (1,)), ((), ())), preferred_element_type=F32
        )
        similar = similar + bias[lo:lo + tile]
        similar = jnp.where(
            iota((tile, SLOTS), 0) + lo == iota((tile, SLOTS), 1), -1.0, similar
        )
        best = jnp.maximum(best, jnp.max(similar, axis=0, keepdims=True))
    spread = jnp.where(iota((N_FINE, SLOTS), 1) // CAP == iota((N_FINE, SLOTS), 0), best, 0.0)
    fold = (iota((SLOTS, CAP), 0) % CAP == iota((SLOTS, CAP), 1)).astype(F32)
    out_ref[...] = high(spread, fold)


def pick_body(label_ref, slot_ref, best_ref, out_ref):
    onehot = (iota((N_FINE, ROW_DEV), 0) == label_ref[...]).astype(F32)
    mine = lax.dot_general(
        best_ref[...], onehot, (((0,), (0,)), ((), ())),
        precision=lax.Precision.HIGHEST, preferred_element_type=F32,
    )
    chosen = iota((CAP, ROW_DEV), 0) == slot_ref[...]
    out_ref[...] = jnp.sum(jnp.where(chosen, mine, 0.0), axis=0, keepdims=True)


def swap(value, axes):
    return lax.all_to_all(value, axes, split_axis=0, concat_axis=0, tiled=True)


def per_device(embeddings, labels):
    label = labels.reshape(1, ROW_DEV)
    strips = call(
        gram_body, jax.ShapeDtypeStruct((D, STRIP), BF16), 2 * ROW_DEV * D * D, 1 << 20, name="gram"
    )(embeddings)
    parts = swap(strips.reshape(N_PLANE, STRIP_ROWS, STRIP), PLANE)

    outgoing, slot = call(
        pack_body,
        (
            jax.ShapeDtypeStruct((SLOTS, D), BF16),
            jax.ShapeDtypeStruct((1, ROW_DEV), jnp.int32),
        ),
        2 * SLOTS * ROW_DEV * D, 2 << 20, name="pack",
    )(label, embeddings)
    received = swap(outgoing.reshape(N_FINE, CAP, D), FINE).reshape(SLOTS, D)

    strip = jnp.sum(parts.astype(F32), axis=0)
    layers = swap(jnp.broadcast_to(strip, (N_Z, STRIP_ROWS, STRIP)), "z")
    strip = jnp.sum(layers, axis=0)
    for axes, differs, _ in DOUBLING:
        size = math.prod(SIZES[AXES.index(axis)] for axis in axes)
        other = lax.ppermute(strip, axes, [(i, i ^ differs) for i in range(size)])
        near, strip = strip, jnp.concatenate([strip, other], axis=0)
    whiten_b = call(
        root_body, jax.ShapeDtypeStruct((D, D), BF16), 36 * D * D * D, 2 << 20,
        (pltpu.VMEM((D, STRIP), F32), pltpu.VMEM((D, D), F32)), name="root",
        specs=(SMEM, VMEM, VMEM),
    )(lax.axis_index(PLANE).reshape(1), near, other)

    best = call(
        best_body, jax.ShapeDtypeStruct((N_FINE, CAP), F32),
        2 * SLOTS * D * (D + SLOTS), 2 << 20, name="best",
    )(received, whiten_b)
    returned = swap(best.reshape(N_FINE, 1, CAP), FINE).reshape(N_FINE, CAP)
    picked = call(
        pick_body, jax.ShapeDtypeStruct((1, ROW_DEV), F32), 1 << 20, 1 << 16, name="pick"
    )(label, slot, returned)
    return picked.reshape(ROW_DEV)


def solution(mesh):
    fine = Mesh(mesh.devices.reshape(SIZES), AXES)
    return jax.shard_map(
        per_device,
        mesh=fine,
        in_specs=(P(AXES, None), P(AXES, None)),
        out_specs=P(AXES),
        check_vma=False,
    )
```

```python
import math

import jax
import jax.numpy as jnp
from jax import lax
from jax.experimental import pallas as pl
from jax.experimental.pallas import tpu as pltpu
from jax.sharding import Mesh, PartitionSpec as P

ITERS = 2
EPS = 1e-06
RIDGE = 0.001

AXES = ("y", "xh", "xl", "z", "c")
SIZES = (8, 2, 2, 16, 2)
FINE = ("xl", "z", "c")
PLANE = ("y", "xh", "xl", "c")

D = 512
ROW_DEV = 512
ROWS = 524288
N_FINE = 64
N_PLANE = 64
N_Z = 16
CAP = 16
SLOTS = N_FINE * CAP
BLOCK = 128
BLOCKS = D // BLOCK
STRIP = 3 * BLOCK
STRIP_ROWS = D // N_PLANE
SHRINK = 2.0 ** -12
DOUBLING = (
    (("y",), 1, 8),
    (("y",), 2, 16),
    (("y",), 4, 32),
    (("xh", "xl"), 3, 6),
    (("xl",), 1, 2),
    (("c",), 1, 1),
)

F32 = jnp.float32
BF16 = jnp.bfloat16


def iota(shape, dim):
    return lax.broadcasted_iota(jnp.int32, shape, dim)


VMEM = pl.BlockSpec(memory_space=pltpu.VMEM)
SMEM = pl.BlockSpec(memory_space=pltpu.SMEM)


def call(body, outs, flops, moved, scratch=(), name=None, specs=None):
    return pl.pallas_call(
        body,
        **({} if specs is None else dict(in_specs=specs)),
        out_shape=outs,
        scratch_shapes=scratch,
        name=name,
        compiler_params=pltpu.CompilerParams(vmem_limit_bytes=48 << 20),
        cost_estimate=pl.CostEstimate(flops=flops, bytes_accessed=moved, transcendentals=0),
    )


def gram_body(rows_ref, out_ref):
    rows = rows_ref[...]
    gram = lax.dot_general(rows, rows, (((0,), (0,)), ((), ())), preferred_element_type=F32)
    for b in range(BLOCKS):
        for k in range(3):
            c = (b + k) % BLOCKS
            out_ref[b * BLOCK:(b + 1) * BLOCK, k * BLOCK:(k + 1) * BLOCK] = gram[
                b * BLOCK:(b + 1) * BLOCK, c * BLOCK:(c + 1) * BLOCK
            ].astype(out_ref.dtype)


def pack_body(label_ref, rows_ref, out_ref, slot_ref):
    label = label_ref[...]
    onehot = (iota((N_FINE, ROW_DEV), 0) == label).astype(F32)
    earlier = (iota((ROW_DEV, ROW_DEV), 0) < iota((ROW_DEV, ROW_DEV), 1)).astype(BF16)
    rank = jnp.dot(onehot.astype(BF16), earlier, preferred_element_type=F32)
    slot = jnp.sum(onehot * rank, axis=0, keepdims=True).astype(jnp.int32)
    slot_ref[...] = slot
    place = label * CAP + slot
    chosen = (iota((SLOTS, ROW_DEV), 0) == place).astype(F32).astype(BF16)
    packed = jnp.dot(chosen, rows_ref[...], preferred_element_type=F32)
    filled = jnp.dot(chosen, jnp.ones((ROW_DEV, BLOCK), BF16), preferred_element_type=F32) > 0.5
    for k in range(D // BLOCK):
        part = packed[:, k * BLOCK:(k + 1) * BLOCK]
        out_ref[:, k * BLOCK:(k + 1) * BLOCK] = jnp.where(filled, part, jnp.nan).astype(BF16)


def high(left, right):
    return jnp.dot(left, right, precision=lax.Precision.HIGHEST, preferred_element_type=F32)


def root_body(me_ref, near_ref, far_ref, out_ref, strip_ref, full_ref):
    half = N_PLANE // 2
    for k in range(N_PLANE):
        differs = 0
        for bit, (_, _, mask) in enumerate(DOUBLING):
            if k >> bit & 1:
                differs ^= mask
        source, at = (near_ref, k) if k < half else (far_ref, k - half)
        to = pl.multiple_of((me_ref[0] ^ differs) * STRIP_ROWS, STRIP_ROWS)
        strip_ref[pl.ds(to, STRIP_ROWS), :] = source[at * STRIP_ROWS:(at + 1) * STRIP_ROWS, :]
    for b in range(BLOCKS):
        for k in range(BLOCKS):
            c = (b + k) % BLOCKS
            if k < 3:
                piece = strip_ref[b * BLOCK:(b + 1) * BLOCK, k * BLOCK:(k + 1) * BLOCK]
            else:
                piece = strip_ref[c * BLOCK:(c + 1) * BLOCK, BLOCK:2 * BLOCK].T
            full_ref[b * BLOCK:(b + 1) * BLOCK, c * BLOCK:(c + 1) * BLOCK] = piece
    identity = (iota((D, D), 0) == iota((D, D), 1)).astype(F32)
    second = full_ref[...] / ROWS + RIDGE * identity
    norm_scale = jnp.max(jnp.sum(jnp.abs(second), axis=0, keepdims=True), axis=1, keepdims=True)
    root_est = second / norm_scale
    inverse_est = 0.5 * (3.0 * identity - root_est)
    root_est = high(root_est, inverse_est)
    newton_step = 0.5 * (3.0 * identity - high(inverse_est, root_est))
    inverse_est = high(newton_step, inverse_est)
    out_ref[...] = (inverse_est / jnp.sqrt(norm_scale)).astype(BF16)


def best_body(rows_ref, whiten_ref, out_ref):
    rows = rows_ref[...].astype(F32)
    present = rows == rows
    clean = jnp.where(present, rows, 0.0).astype(BF16)
    whitened = jnp.dot(clean, whiten_ref[...], preferred_element_type=F32)
    meansq = jnp.mean(whitened * whitened, axis=-1, keepdims=True)
    unit = (whitened * lax.rsqrt(D * (meansq + EPS))).astype(BF16)
    bias = jnp.where(present[:, :1], 0.0, -4.0)
    tile = 256
    best = jnp.full((1, SLOTS), -1.0, F32)
    for b in range(SLOTS // tile):
        lo = b * tile
        similar = lax.dot_general(
            unit[lo:lo + tile], unit, (((1,), (1,)), ((), ())), preferred_element_type=F32
        )
        similar = similar + bias[lo:lo + tile]
        similar = jnp.where(
            iota((tile, SLOTS), 0) + lo == iota((tile, SLOTS), 1), -1.0, similar
        )
        best = jnp.maximum(best, jnp.max(similar, axis=0, keepdims=True))
    spread = jnp.where(iota((N_FINE, SLOTS), 1) // CAP == iota((N_FINE, SLOTS), 0), best, 0.0)
    fold = (iota((SLOTS, CAP), 0) % CAP == iota((SLOTS, CAP), 1)).astype(F32)
    out_ref[...] = high(spread, fold)


def pick_body(label_ref, slot_ref, best_ref, out_ref):
    onehot = (iota((N_FINE, ROW_DEV), 0) == label_ref[...]).astype(F32)
    mine = lax.dot_general(
        best_ref[...], onehot, (((0,), (0,)), ((), ())),
        precision=lax.Precision.HIGHEST, preferred_element_type=F32,
    )
    chosen = iota((CAP, ROW_DEV), 0) == slot_ref[...]
    out_ref[...] = jnp.sum(jnp.where(chosen, mine, 0.0), axis=0, keepdims=True)


def swap(value, axes):
    return lax.all_to_all(value, axes, split_axis=0, concat_axis=0, tiled=True)


def per_device(embeddings, labels):
    label = labels.reshape(1, ROW_DEV)
    strips = call(
        gram_body, jax.ShapeDtypeStruct((D, STRIP), BF16), 2 * ROW_DEV * D * D, 1 << 20, name="gram"
    )(embeddings)
    parts = swap(strips.reshape(N_PLANE, STRIP_ROWS, STRIP), PLANE)

    outgoing, slot = call(
        pack_body,
        (
            jax.ShapeDtypeStruct((SLOTS, D), BF16),
            jax.ShapeDtypeStruct((1, ROW_DEV), jnp.int32),
        ),
        2 * SLOTS * ROW_DEV * D, 2 << 20, name="pack",
    )(label, embeddings)
    received = swap(outgoing.reshape(N_FINE, CAP, D), FINE).reshape(SLOTS, D)

    strip = (jnp.sum(parts.astype(F32), axis=0) * SHRINK).astype(jnp.float16)
    layers = swap(jnp.broadcast_to(strip, (N_Z, STRIP_ROWS, STRIP)), "z")
    strip = jnp.sum(layers.astype(F32), axis=0) * (1.0 / SHRINK)
    for axes, differs, _ in DOUBLING:
        size = math.prod(SIZES[AXES.index(axis)] for axis in axes)
        other = lax.ppermute(strip, axes, [(i, i ^ differs) for i in range(size)])
        near, strip = strip, jnp.concatenate([strip, other], axis=0)
    whiten_b = call(
        root_body, jax.ShapeDtypeStruct((D, D), BF16), 36 * D * D * D, 2 << 20,
        (pltpu.VMEM((D, STRIP), F32), pltpu.VMEM((D, D), F32)), name="root",
        specs=(SMEM, VMEM, VMEM),
    )(lax.axis_index(PLANE).reshape(1), near, other)

    best = call(
        best_body, jax.ShapeDtypeStruct((N_FINE, CAP), F32),
        2 * SLOTS * D * (D + SLOTS), 2 << 20, name="best",
    )(received, whiten_b)
    returned = swap(best.reshape(N_FINE, 1, CAP), FINE).reshape(N_FINE, CAP)
    picked = call(
        pick_body, jax.ShapeDtypeStruct((1, ROW_DEV), F32), 1 << 20, 1 << 16, name="pick"
    )(label, slot, returned)
    return picked.reshape(ROW_DEV)


def solution(mesh):
    fine = Mesh(mesh.devices.reshape(SIZES), AXES)
    return jax.shard_map(
        per_device,
        mesh=fine,
        in_specs=(P(AXES, None), P(AXES, None)),
        out_specs=P(AXES),
        check_vma=False,
    )
```

```python
import math

import jax
import jax.numpy as jnp
from jax import lax
from jax.experimental import pallas as pl
from jax.experimental.pallas import tpu as pltpu
from jax.sharding import Mesh, PartitionSpec as P

ITERS = 2
EPS = 1e-06
RIDGE = 0.001

AXES = ("y", "xh", "xl", "z", "c")
SIZES = (8, 2, 2, 16, 2)
FINE = ("xl", "z", "c")
FLAT = ("y", "xh", "xl")
PLANE = ("c",) + FLAT

D = 512
ROW_DEV = 512
ROWS = 524288
N_FINE = 64
N_PLANE = 64
N_Z = 16
CAP = 16
SLOTS = N_FINE * CAP
BLOCK = 128
BLOCKS = D // BLOCK
HALF = D // 2
PARTS = 4

STRIP = 3 * BLOCK
STRIP_ROWS = D // N_PLANE
SHRINK = 2.0 ** -12
DOUBLING = (
    (("y",), 1, 4),
    (("y",), 2, 8),
    (("y",), 4, 16),
    (("xh", "xl"), 3, 3),
    (("xl",), 1, 1),
    (("c",), 1, 32),
)

F32 = jnp.float32
BF16 = jnp.bfloat16


def iota(shape, dim):
    return lax.broadcasted_iota(jnp.int32, shape, dim)


VMEM = pl.BlockSpec(memory_space=pltpu.VMEM)
SMEM = pl.BlockSpec(memory_space=pltpu.SMEM)


def call(body, outs, flops, moved, scratch=(), name=None, specs=None, room=48):
    return pl.pallas_call(
        body,
        **({} if specs is None else dict(in_specs=specs)),
        out_shape=outs,
        scratch_shapes=scratch,
        name=name,
        compiler_params=pltpu.CompilerParams(vmem_limit_bytes=room << 20),
        cost_estimate=pl.CostEstimate(flops=flops, bytes_accessed=moved, transcendentals=0),
    )


def gram_body(rows_ref, out_ref, held_ref, sems):
    part = ROW_DEV // PARTS
    copies = [
        pltpu.make_async_copy(
            rows_ref.at[pl.ds(i * part, part), :], held_ref.at[pl.ds(i * part, part), :], sems.at[i]
        )
        for i in range(PARTS)
    ]
    for copy in copies:
        copy.start()
    for copy in copies:
        copy.wait()
    rows = held_ref[...]
    gram = lax.dot_general(rows, rows, (((0,), (0,)), ((), ())), preferred_element_type=F32)
    for b in range(BLOCKS):
        for k in range(3):
            c = (b + k) % BLOCKS
            out_ref[b * BLOCK:(b + 1) * BLOCK, k * BLOCK:(k + 1) * BLOCK] = gram[
                b * BLOCK:(b + 1) * BLOCK, c * BLOCK:(c + 1) * BLOCK
            ].astype(out_ref.dtype)


def halve_body(core_ref, both_ref, out_ref):
    at = pl.multiple_of(core_ref[0] * HALF, HALF)
    out_ref[...] = (
        both_ref[pl.ds(at, HALF), :].astype(F32) + both_ref[pl.ds(at + D, HALF), :].astype(F32)
    ).astype(BF16)


def pack_body(label_ref, rows_ref, out_ref, slot_ref):
    label = label_ref[...]
    onehot = (iota((N_FINE, ROW_DEV), 0) == label).astype(F32)
    earlier = (iota((ROW_DEV, ROW_DEV), 0) < iota((ROW_DEV, ROW_DEV), 1)).astype(BF16)
    rank = jnp.dot(onehot.astype(BF16), earlier, preferred_element_type=F32)
    slot = jnp.sum(onehot * rank, axis=0, keepdims=True).astype(jnp.int32)
    slot_ref[...] = slot
    place = label * CAP + slot
    chosen = (iota((SLOTS, ROW_DEV), 0) == place).astype(F32).astype(BF16)
    packed = jnp.dot(chosen, rows_ref[...], preferred_element_type=F32)
    filled = jnp.dot(chosen, jnp.ones((ROW_DEV, BLOCK), BF16), preferred_element_type=F32) > 0.5
    for k in range(D // BLOCK):
        part = packed[:, k * BLOCK:(k + 1) * BLOCK]
        out_ref[:, k * BLOCK:(k + 1) * BLOCK] = jnp.where(filled, part, jnp.nan).astype(BF16)


def high(left, right):
    return jnp.dot(left, right, precision=lax.Precision.HIGHEST, preferred_element_type=F32)


def root_body(me_ref, near_ref, far_ref, out_ref, strip_ref, full_ref):
    half = N_PLANE // 2
    for k in range(N_PLANE):
        differs = 0
        for bit, (_, _, mask) in enumerate(DOUBLING):
            if k >> bit & 1:
                differs ^= mask
        source, at = (near_ref, k) if k < half else (far_ref, k - half)
        to = pl.multiple_of((me_ref[0] ^ differs) * STRIP_ROWS, STRIP_ROWS)
        strip_ref[pl.ds(to, STRIP_ROWS), :] = source[at * STRIP_ROWS:(at + 1) * STRIP_ROWS, :]
    for b in range(BLOCKS):
        for k in range(BLOCKS):
            c = (b + k) % BLOCKS
            if k < 3:
                piece = strip_ref[b * BLOCK:(b + 1) * BLOCK, k * BLOCK:(k + 1) * BLOCK]
            else:
                piece = strip_ref[c * BLOCK:(c + 1) * BLOCK, BLOCK:2 * BLOCK].T
            full_ref[b * BLOCK:(b + 1) * BLOCK, c * BLOCK:(c + 1) * BLOCK] = piece
    identity = (iota((D, D), 0) == iota((D, D), 1)).astype(F32)
    second = full_ref[...] / ROWS + RIDGE * identity
    norm_scale = jnp.max(jnp.sum(jnp.abs(second), axis=0, keepdims=True), axis=1, keepdims=True)
    root_est = second / norm_scale
    inverse_est = 0.5 * (3.0 * identity - root_est)
    root_est = high(root_est, inverse_est)
    newton_step = 0.5 * (3.0 * identity - high(inverse_est, root_est))
    inverse_est = high(newton_step, inverse_est)
    out_ref[...] = (inverse_est / jnp.sqrt(norm_scale)).astype(BF16)


def best_body(rows_ref, whiten_ref, out_ref):
    rows = rows_ref[...].astype(F32)
    present = rows == rows
    clean = jnp.where(present, rows, 0.0).astype(BF16)
    whitened = jnp.dot(clean, whiten_ref[...], preferred_element_type=F32)
    meansq = jnp.mean(whitened * whitened, axis=-1, keepdims=True)
    unit = (whitened * lax.rsqrt(D * (meansq + EPS))).astype(BF16)
    bias = jnp.where(present[:, :1], 0.0, -4.0)
    tile = 256
    own = iota((tile, tile), 0) == iota((tile, tile), 1)
    columns = []
    for c in range(SLOTS // tile):
        best = jnp.full((1, tile), -1.0, F32)
        for b in range(SLOTS // tile):
            similar = lax.dot_general(
                unit[b * tile:(b + 1) * tile], unit[c * tile:(c + 1) * tile],
                (((1,), (1,)), ((), ())), preferred_element_type=F32,
            ) + bias[b * tile:(b + 1) * tile]
            if b == c:
                similar = jnp.where(own, -1.0, similar)
            best = jnp.maximum(best, jnp.max(similar, axis=0, keepdims=True))
        columns.append(best)
    best = jnp.concatenate(columns, axis=1)
    spread = jnp.where(iota((N_FINE, SLOTS), 1) // CAP == iota((N_FINE, SLOTS), 0), best, 0.0)
    fold = (iota((SLOTS, CAP), 0) % CAP == iota((SLOTS, CAP), 1)).astype(F32)
    out_ref[...] = high(spread, fold)


def pick_body(label_ref, slot_ref, best_ref, out_ref):
    onehot = (iota((N_FINE, ROW_DEV), 0) == label_ref[...]).astype(F32)
    mine = lax.dot_general(
        best_ref[...], onehot, (((0,), (0,)), ((), ())),
        precision=lax.Precision.HIGHEST, preferred_element_type=F32,
    )
    chosen = iota((CAP, ROW_DEV), 0) == slot_ref[...]
    out_ref[...] = jnp.sum(jnp.where(chosen, mine, 0.0), axis=0, keepdims=True)


def swap(value, axes):
    return lax.all_to_all(value, axes, split_axis=0, concat_axis=0, tiled=True)


def per_device(embeddings, labels):
    label = labels.reshape(1, ROW_DEV)
    strips = call(
        gram_body, jax.ShapeDtypeStruct((D, STRIP), BF16), 2 * ROW_DEV * D * D, 1 << 20,
        (pltpu.VMEM((ROW_DEV, D), BF16), pltpu.SemaphoreType.DMA((PARTS,))), name="gram",
        specs=(pl.BlockSpec(memory_space=pltpu.HBM),),
    )(pltpu.with_memory_space_constraint(embeddings, pltpu.HBM))
    both = lax.all_gather(strips, "c", axis=0, tiled=True)
    strips = call(
        halve_body, jax.ShapeDtypeStruct((HALF, STRIP), BF16), D * STRIP, 1 << 20, name="halve",
        specs=(SMEM, VMEM),
    )(lax.axis_index("c").reshape(1), both)
    parts = swap(strips.reshape(N_PLANE // 2, STRIP_ROWS, STRIP), FLAT)

    outgoing, slot = call(
        pack_body,
        (
            jax.ShapeDtypeStruct((SLOTS, D), BF16),
            jax.ShapeDtypeStruct((1, ROW_DEV), jnp.int32),
        ),
        2 * SLOTS * ROW_DEV * D, 2 << 20, name="pack",
    )(label, embeddings)
    received = swap(outgoing.reshape(N_FINE, CAP, D), FINE).reshape(SLOTS, D)

    strip = (jnp.sum(parts.astype(F32), axis=0) * SHRINK).astype(jnp.float16)
    layers = swap(jnp.broadcast_to(strip, (N_Z, STRIP_ROWS, STRIP)), "z")
    strip = jnp.sum(layers.astype(F32), axis=0) * (1.0 / SHRINK)
    for axes, differs, _ in DOUBLING:
        size = math.prod(SIZES[AXES.index(axis)] for axis in axes)
        other = lax.ppermute(strip, axes, [(i, i ^ differs) for i in range(size)])
        near, strip = strip, jnp.concatenate([strip, other], axis=0)
    whiten_b = call(
        root_body, jax.ShapeDtypeStruct((D, D), BF16), 36 * D * D * D, 2 << 20,
        (pltpu.VMEM((D, STRIP), F32), pltpu.VMEM((D, D), F32)), name="root",
        specs=(SMEM, VMEM, VMEM),
    )(lax.axis_index(PLANE).reshape(1), near, other)

    best = call(
        best_body, jax.ShapeDtypeStruct((N_FINE, CAP), F32),
        2 * SLOTS * D * (D + SLOTS), 2 << 20, name="best",
    )(received, whiten_b)
    returned = swap(best.reshape(N_FINE, 1, CAP), FINE).reshape(N_FINE, CAP)
    picked = call(
        pick_body, jax.ShapeDtypeStruct((1, ROW_DEV), F32), 1 << 20, 1 << 16, name="pick"
    )(label, slot, returned)
    return picked.reshape(ROW_DEV)


def solution(mesh):
    fine = Mesh(mesh.devices.reshape(SIZES), AXES)
    return jax.shard_map(
        per_device,
        mesh=fine,
        in_specs=(P(AXES, None), P(AXES, None)),
        out_specs=P(AXES),
        check_vma=False,
    )
```

```python
import math

import jax
import jax.numpy as jnp
from jax import lax
from jax.experimental import pallas as pl
from jax.experimental.pallas import tpu as pltpu
from jax.sharding import Mesh, PartitionSpec as P

ITERS = 2
EPS = 1e-06
RIDGE = 0.001

AXES = ("y", "xh", "xl", "z", "c")
SIZES = (8, 2, 2, 16, 2)
FINE = ("xl", "z", "c")
FLAT = ("y", "xh", "xl")
PLANE = ("c",) + FLAT

D = 512
ROW_DEV = 512
ROWS = 524288
N_FINE = 64
N_PLANE = 64
N_Z = 16
CAP = 16
SLOTS = N_FINE * CAP
BLOCK = 128
BLOCKS = D // BLOCK
HALF = D // 2
PARTS = 2

STRIP = 3 * BLOCK
STRIP_ROWS = D // N_PLANE
SHRINK = 2.0 ** -12
CHIP_SHRINK = 2.0 ** -7
DOUBLING = (
    (("y",), 1, 4),
    (("y",), 2, 8),
    (("y",), 4, 16),
    (("xh", "xl"), 3, 3),
    (("xl",), 1, 1),
    (("c",), 1, 32),
)

F32 = jnp.float32
BF16 = jnp.bfloat16
F16 = jnp.float16


def iota(shape, dim):
    return lax.broadcasted_iota(jnp.int32, shape, dim)


VMEM = pl.BlockSpec(memory_space=pltpu.VMEM)
SMEM = pl.BlockSpec(memory_space=pltpu.SMEM)


def call(body, outs, flops, moved, scratch=(), name=None, specs=None, room=48):
    return pl.pallas_call(
        body,
        **({} if specs is None else dict(in_specs=specs)),
        out_shape=outs,
        scratch_shapes=scratch,
        name=name,
        compiler_params=pltpu.CompilerParams(vmem_limit_bytes=room << 20),
        cost_estimate=pl.CostEstimate(flops=flops, bytes_accessed=moved, transcendentals=0),
    )


def gram_body(rows_ref, out_ref, held_ref, sems):
    part = ROW_DEV // PARTS
    copies = [
        pltpu.make_async_copy(
            rows_ref.at[pl.ds(i * part, part), :], held_ref.at[pl.ds(i * part, part), :], sems.at[i]
        )
        for i in range(PARTS)
    ]
    for copy in copies:
        copy.start()
    gram = None
    for i, copy in enumerate(copies):
        copy.wait()
        rows = held_ref[i * part:(i + 1) * part, :]
        term = lax.dot_general(rows, rows, (((0,), (0,)), ((), ())), preferred_element_type=F32)
        gram = term if gram is None else gram + term
    for b in range(BLOCKS):
        for k in range(3):
            c = (b + k) % BLOCKS
            out_ref[b * BLOCK:(b + 1) * BLOCK, k * BLOCK:(k + 1) * BLOCK] = gram[
                b * BLOCK:(b + 1) * BLOCK, c * BLOCK:(c + 1) * BLOCK
            ].astype(out_ref.dtype)


def pack_body(label_ref, rows_ref, out_ref, slot_ref):
    label = label_ref[...]
    onehot = (iota((N_FINE, ROW_DEV), 0) == label).astype(F32)
    earlier = (iota((ROW_DEV, ROW_DEV), 0) < iota((ROW_DEV, ROW_DEV), 1)).astype(BF16)
    rank = jnp.dot(onehot.astype(BF16), earlier, preferred_element_type=F32)
    slot = jnp.sum(onehot * rank, axis=0, keepdims=True).astype(jnp.int32)
    slot_ref[...] = slot
    place = label * CAP + slot
    chosen = (iota((SLOTS, ROW_DEV), 0) == place).astype(F32).astype(BF16)
    packed = jnp.dot(chosen, rows_ref[...], preferred_element_type=F32)
    filled = jnp.dot(chosen, jnp.ones((ROW_DEV, BLOCK), BF16), preferred_element_type=F32) > 0.5
    for k in range(D // BLOCK):
        part = packed[:, k * BLOCK:(k + 1) * BLOCK]
        out_ref[:, k * BLOCK:(k + 1) * BLOCK] = jnp.where(filled, part, jnp.nan).astype(BF16)


def high(left, right):
    return jnp.dot(left, right, precision=lax.Precision.HIGHEST, preferred_element_type=F32)


def root_body(me_ref, near_ref, far_ref, out_ref, strip_ref, full_ref):
    half = N_PLANE // 2
    for k in range(N_PLANE):
        differs = 0
        for bit, (_, _, mask) in enumerate(DOUBLING):
            if k >> bit & 1:
                differs ^= mask
        source, at = (near_ref, k) if k < half else (far_ref, k - half)
        to = pl.multiple_of((me_ref[0] ^ differs) * STRIP_ROWS, STRIP_ROWS)
        strip_ref[pl.ds(to, STRIP_ROWS), :] = source[at * STRIP_ROWS:(at + 1) * STRIP_ROWS, :]
    for b in range(BLOCKS):
        for k in range(BLOCKS):
            c = (b + k) % BLOCKS
            if k < 3:
                piece = strip_ref[b * BLOCK:(b + 1) * BLOCK, k * BLOCK:(k + 1) * BLOCK]
            else:
                piece = strip_ref[c * BLOCK:(c + 1) * BLOCK, BLOCK:2 * BLOCK].T
            full_ref[b * BLOCK:(b + 1) * BLOCK, c * BLOCK:(c + 1) * BLOCK] = piece
    identity = (iota((D, D), 0) == iota((D, D), 1)).astype(F32)
    second = full_ref[...] / ROWS + RIDGE * identity
    norm_scale = jnp.max(jnp.sum(jnp.abs(second), axis=0, keepdims=True), axis=1, keepdims=True)
    root_est = second / norm_scale
    inverse_est = 0.5 * (3.0 * identity - root_est)
    root_est = high(root_est, inverse_est)
    newton_step = 0.5 * (3.0 * identity - high(inverse_est, root_est))
    inverse_est = high(newton_step, inverse_est)
    out_ref[...] = (inverse_est / jnp.sqrt(norm_scale)).astype(BF16)


def best_body(rows_ref, whiten_ref, out_ref):
    rows = rows_ref[...].astype(F32)
    present = rows == rows
    clean = jnp.where(present, rows, 0.0).astype(BF16)
    whitened = jnp.dot(clean, whiten_ref[...], preferred_element_type=F32)
    meansq = jnp.mean(whitened * whitened, axis=-1, keepdims=True)
    unit = (whitened * lax.rsqrt(D * (meansq + EPS))).astype(BF16)
    bias = jnp.where(present[:, :1], 0.0, -4.0)
    tile = 256
    own = iota((tile, tile), 0) == iota((tile, tile), 1)
    columns = []
    for c in range(SLOTS // tile):
        best = jnp.full((1, tile), -1.0, F32)
        for b in range(SLOTS // tile):
            similar = lax.dot_general(
                unit[b * tile:(b + 1) * tile], unit[c * tile:(c + 1) * tile],
                (((1,), (1,)), ((), ())), preferred_element_type=F32,
            ) + bias[b * tile:(b + 1) * tile]
            if b == c:
                similar = jnp.where(own, -1.0, similar)
            best = jnp.maximum(best, jnp.max(similar, axis=0, keepdims=True))
        columns.append(best)
    best = jnp.concatenate(columns, axis=1)
    for source in range(N_FINE):
        out_ref[source:source + 1, :] = best[:, source * CAP:(source + 1) * CAP]


def pick_body(label_ref, slot_ref, best_ref, out_ref):
    onehot = (iota((N_FINE, ROW_DEV), 0) == label_ref[...]).astype(F32)
    mine = lax.dot_general(
        best_ref[...], onehot, (((0,), (0,)), ((), ())),
        precision=lax.Precision.HIGHEST, preferred_element_type=F32,
    )
    chosen = iota((CAP, ROW_DEV), 0) == slot_ref[...]
    out_ref[...] = jnp.sum(jnp.where(chosen, mine, 0.0), axis=0, keepdims=True)


def swap(value, axes):
    return lax.all_to_all(value, axes, split_axis=0, concat_axis=0, tiled=True)


def per_device(embeddings, labels):
    label = labels.reshape(1, ROW_DEV)
    strips = call(
        gram_body, jax.ShapeDtypeStruct((D, STRIP), BF16), 2 * ROW_DEV * D * D, 1 << 20,
        (pltpu.VMEM((ROW_DEV, D), BF16), pltpu.SemaphoreType.DMA((PARTS,))), name="gram",
        specs=(pl.BlockSpec(memory_space=pltpu.HBM),),
    )(pltpu.with_memory_space_constraint(embeddings, pltpu.HBM))
    both = lax.all_gather(strips, "c", axis=0, tiled=True)
    at = lax.axis_index("c") * HALF
    strips = sum(
        lax.dynamic_slice(
            both, (start, 0), (HALF, STRIP), allow_negative_indices=False
        ).astype(F32)
        for start in (at, at + D)
    )
    strips = (strips * CHIP_SHRINK).astype(F16)
    parts = swap(strips.reshape(N_PLANE // 2, STRIP_ROWS, STRIP), FLAT)

    outgoing, slot = call(
        pack_body,
        (
            jax.ShapeDtypeStruct((SLOTS, D), BF16),
            jax.ShapeDtypeStruct((1, ROW_DEV), jnp.int32),
        ),
        2 * SLOTS * ROW_DEV * D, 2 << 20, name="pack",
    )(label, embeddings)
    received = swap(outgoing.reshape(N_FINE, CAP, D), FINE).reshape(SLOTS, D)

    strip = (jnp.sum(parts.astype(F32), axis=0) * (SHRINK / CHIP_SHRINK)).astype(F16)
    layers = swap(jnp.broadcast_to(strip, (N_Z, STRIP_ROWS, STRIP)), "z")
    strip = jnp.sum(layers.astype(F32), axis=0) * (1.0 / SHRINK)
    for axes, differs, _ in DOUBLING:
        size = math.prod(SIZES[AXES.index(axis)] for axis in axes)
        other = lax.ppermute(strip, axes, [(i, i ^ differs) for i in range(size)])
        near, strip = strip, jnp.concatenate([strip, other], axis=0)
    whiten_b = call(
        root_body, jax.ShapeDtypeStruct((D, D), BF16), 36 * D * D * D, 2 << 20,
        (pltpu.VMEM((D, STRIP), F32), pltpu.VMEM((D, D), F32)), name="root",
        specs=(SMEM, VMEM, VMEM),
    )(lax.axis_index(PLANE).reshape(1), near, other)

    best = call(
        best_body, jax.ShapeDtypeStruct((N_FINE, CAP), F32),
        2 * SLOTS * D * (D + SLOTS), 2 << 20, name="best",
    )(received, whiten_b)
    returned = swap(best.reshape(N_FINE, 1, CAP), FINE).reshape(N_FINE, CAP)
    picked = call(
        pick_body, jax.ShapeDtypeStruct((1, ROW_DEV), F32), 1 << 20, 1 << 16, name="pick"
    )(label, slot, returned)
    return picked.reshape(ROW_DEV)


def solution(mesh):
    fine = Mesh(mesh.devices.reshape(SIZES), AXES)
    return jax.shard_map(
        per_device,
        mesh=fine,
        in_specs=(P(AXES, None), P(AXES, None)),
        out_specs=P(AXES),
        check_vma=False,
    )
```

```python
import math

import jax
import jax.numpy as jnp
from jax import lax
from jax.experimental import pallas as pl
from jax.experimental.pallas import tpu as pltpu
from jax.sharding import Mesh, PartitionSpec as P

ITERS = 2
EPS = 1e-06
RIDGE = 0.001

AXES = ("y", "xh", "xl", "z", "c")
SIZES = (8, 2, 2, 16, 2)
FINE = ("xl", "z", "c")
FLAT = ("y", "xh", "xl")
PLANE = ("c",) + FLAT

D = 512
ROW_DEV = 512
ROWS = 524288
N_FINE = 64
N_PLANE = 64
N_Z = 16
CAP = 16
SLOTS = N_FINE * CAP
BLOCK = 128
BLOCKS = D // BLOCK
HALF = D // 2
PARTS = 2

STRIP = 3 * BLOCK
STRIP_ROWS = D // N_PLANE
SHRINK = 2.0 ** -12
CHIP_SHRINK = 2.0 ** -7
DOUBLING = (
    (("y",), 1, 4),
    (("y",), 2, 8),
    (("y",), 4, 16),
    (("xh", "xl"), 3, 3),
    (("xl",), 1, 1),
    (("c",), 1, 32),
)

F32 = jnp.float32
BF16 = jnp.bfloat16
F16 = jnp.float16


def iota(shape, dim):
    return lax.broadcasted_iota(jnp.int32, shape, dim)


VMEM = pl.BlockSpec(memory_space=pltpu.VMEM)
SMEM = pl.BlockSpec(memory_space=pltpu.SMEM)


def call(body, outs, flops, moved, scratch=(), name=None, specs=None, room=48):
    return pl.pallas_call(
        body,
        **({} if specs is None else dict(in_specs=specs)),
        out_shape=outs,
        scratch_shapes=scratch,
        name=name,
        compiler_params=pltpu.CompilerParams(vmem_limit_bytes=room << 20),
        cost_estimate=pl.CostEstimate(flops=flops, bytes_accessed=moved, transcendentals=0),
    )


def gram_body(rows_ref, out_ref, held_ref, sems):
    part = ROW_DEV // PARTS
    copies = [
        pltpu.make_async_copy(
            rows_ref.at[pl.ds(i * part, part), :], held_ref.at[pl.ds(i * part, part), :], sems.at[i]
        )
        for i in range(PARTS)
    ]
    for copy in copies:
        copy.start()
    gram = None
    for i, copy in enumerate(copies):
        copy.wait()
        rows = held_ref[i * part:(i + 1) * part, :]
        term = lax.dot_general(rows, rows, (((0,), (0,)), ((), ())), preferred_element_type=F32)
        gram = term if gram is None else gram + term
    for b in range(BLOCKS):
        for k in range(3):
            c = (b + k) % BLOCKS
            out_ref[b * BLOCK:(b + 1) * BLOCK, k * BLOCK:(k + 1) * BLOCK] = gram[
                b * BLOCK:(b + 1) * BLOCK, c * BLOCK:(c + 1) * BLOCK
            ].astype(out_ref.dtype)


def pack_body(label_ref, rows_ref, out_ref, slot_ref):
    label = label_ref[...]
    onehot = (iota((N_FINE, ROW_DEV), 0) == label).astype(F32)
    earlier = (iota((ROW_DEV, ROW_DEV), 0) < iota((ROW_DEV, ROW_DEV), 1)).astype(BF16)
    rank = jnp.dot(onehot.astype(BF16), earlier, preferred_element_type=F32)
    slot = jnp.sum(onehot * rank, axis=0, keepdims=True).astype(jnp.int32)
    slot_ref[...] = slot
    place = label * CAP + slot
    chosen = (iota((SLOTS, ROW_DEV), 0) == place).astype(F32).astype(BF16)
    packed = jnp.dot(chosen, rows_ref[...], preferred_element_type=F32)
    filled = jnp.dot(chosen, jnp.ones((ROW_DEV, BLOCK), BF16), preferred_element_type=F32) > 0.5
    for k in range(D // BLOCK):
        part = packed[:, k * BLOCK:(k + 1) * BLOCK]
        out_ref[:, k * BLOCK:(k + 1) * BLOCK] = jnp.where(filled, part, jnp.nan).astype(BF16)


def high(left, right):
    return jnp.dot(left, right, precision=lax.Precision.HIGHEST, preferred_element_type=F32)


def root_body(me_ref, near_ref, far_ref, out_ref, strip_ref, full_ref):
    half = N_PLANE // 2
    for k in range(N_PLANE):
        differs = 0
        for bit, (_, _, mask) in enumerate(DOUBLING):
            if k >> bit & 1:
                differs ^= mask
        source, at = (near_ref, k) if k < half else (far_ref, k - half)
        to = pl.multiple_of((me_ref[0] ^ differs) * STRIP_ROWS, STRIP_ROWS)
        strip_ref[pl.ds(to, STRIP_ROWS), :] = source[at * STRIP_ROWS:(at + 1) * STRIP_ROWS, :]
    for b in range(BLOCKS):
        for k in range(BLOCKS):
            c = (b + k) % BLOCKS
            if k < 3:
                piece = strip_ref[b * BLOCK:(b + 1) * BLOCK, k * BLOCK:(k + 1) * BLOCK]
            else:
                piece = strip_ref[c * BLOCK:(c + 1) * BLOCK, BLOCK:2 * BLOCK].T
            full_ref[b * BLOCK:(b + 1) * BLOCK, c * BLOCK:(c + 1) * BLOCK] = piece
    identity = (iota((D, D), 0) == iota((D, D), 1)).astype(F32)
    second = full_ref[...] / ROWS + RIDGE * identity
    norm_scale = jnp.max(jnp.sum(jnp.abs(second), axis=0, keepdims=True), axis=1, keepdims=True)
    root_est = second / norm_scale
    inverse_est = 0.5 * (3.0 * identity - root_est)
    root_est = high(root_est, inverse_est)
    newton_step = 0.5 * (3.0 * identity - high(inverse_est, root_est))
    inverse_est = high(newton_step, inverse_est)
    out_ref[...] = (inverse_est / jnp.sqrt(norm_scale)).astype(BF16)


def best_body(rows_ref, whiten_ref, out_ref):
    present = rows_ref[:, :BLOCK].astype(F32)[:, :1]
    present = present == present
    whitened = jnp.dot(rows_ref[...], whiten_ref[...], preferred_element_type=F32)
    meansq = jnp.mean(whitened * whitened, axis=-1, keepdims=True)
    unit = (whitened * lax.rsqrt(D * (meansq + EPS))).astype(BF16)
    tile = 256
    own = iota((tile, tile), 0) == iota((tile, tile), 1)
    columns = []
    for c in range(SLOTS // tile):
        best = jnp.full((1, tile), -1.0, F32)
        for b in range(SLOTS // tile):
            similar = lax.dot_general(
                unit[b * tile:(b + 1) * tile], unit[c * tile:(c + 1) * tile],
                (((1,), (1,)), ((), ())), preferred_element_type=F32,
            )
            keep = present[b * tile:(b + 1) * tile]
            if b == c:
                keep = keep & jnp.logical_not(own)
            similar = jnp.where(keep, similar, -1.0)
            best = jnp.maximum(best, jnp.max(similar, axis=0, keepdims=True))
        columns.append(best)
    best = jnp.concatenate(columns, axis=1)
    best = jnp.where(best == best, best, -1.0)
    for source in range(N_FINE):
        out_ref[source:source + 1, :] = best[:, source * CAP:(source + 1) * CAP]


def pick_body(label_ref, slot_ref, best_ref, out_ref):
    onehot = (iota((N_FINE, ROW_DEV), 0) == label_ref[...]).astype(F32)
    mine = lax.dot_general(
        best_ref[...], onehot, (((0,), (0,)), ((), ())),
        precision=lax.Precision.HIGHEST, preferred_element_type=F32,
    )
    chosen = iota((CAP, ROW_DEV), 0) == slot_ref[...]
    out_ref[...] = jnp.sum(jnp.where(chosen, mine, 0.0), axis=0, keepdims=True)


def swap(value, axes):
    return lax.all_to_all(value, axes, split_axis=0, concat_axis=0, tiled=True)


def per_device(embeddings, labels):
    label = labels.reshape(1, ROW_DEV)
    strips = call(
        gram_body, jax.ShapeDtypeStruct((D, STRIP), BF16), 2 * ROW_DEV * D * D, 1 << 20,
        (pltpu.VMEM((ROW_DEV, D), BF16), pltpu.SemaphoreType.DMA((PARTS,))), name="gram",
        specs=(pl.BlockSpec(memory_space=pltpu.HBM),),
    )(pltpu.with_memory_space_constraint(embeddings, pltpu.HBM))
    both = lax.all_gather(strips, "c", axis=0, tiled=True)
    at = lax.axis_index("c") * HALF
    strips = sum(
        lax.dynamic_slice(
            both, (start, 0), (HALF, STRIP), allow_negative_indices=False
        ).astype(F32)
        for start in (at, at + D)
    )
    strips = (strips * CHIP_SHRINK).astype(F16)
    parts = swap(strips.reshape(N_PLANE // 2, STRIP_ROWS, STRIP), FLAT)

    outgoing, slot = call(
        pack_body,
        (
            jax.ShapeDtypeStruct((SLOTS, D), BF16),
            jax.ShapeDtypeStruct((1, ROW_DEV), jnp.int32),
        ),
        2 * SLOTS * ROW_DEV * D, 2 << 20, name="pack",
    )(label, embeddings)
    parts, outgoing = lax.optimization_barrier((parts, outgoing))
    received = swap(outgoing.reshape(N_FINE, CAP, D), FINE).reshape(SLOTS, D)

    strip = (jnp.sum(parts.astype(F32), axis=0) * (SHRINK / CHIP_SHRINK)).astype(F16)
    layers = swap(jnp.broadcast_to(strip, (N_Z, STRIP_ROWS, STRIP)), "z")
    strip = jnp.sum(layers.astype(F32), axis=0) * (1.0 / SHRINK)
    for axes, differs, _ in DOUBLING:
        size = math.prod(SIZES[AXES.index(axis)] for axis in axes)
        other = lax.ppermute(strip, axes, [(i, i ^ differs) for i in range(size)])
        near, strip = strip, jnp.concatenate([strip, other], axis=0)
    whiten_b = call(
        root_body, jax.ShapeDtypeStruct((D, D), BF16), 36 * D * D * D, 2 << 20,
        (pltpu.VMEM((D, STRIP), F32), pltpu.VMEM((D, D), F32)), name="root",
        specs=(SMEM, VMEM, VMEM),
    )(lax.axis_index(PLANE).reshape(1), near, other)

    best = call(
        best_body, jax.ShapeDtypeStruct((N_FINE, CAP), F32),
        2 * SLOTS * D * (D + SLOTS), 2 << 20, name="best",
    )(received, whiten_b)
    returned = swap(best.reshape(N_FINE, 1, CAP), FINE).reshape(N_FINE, CAP)
    picked = call(
        pick_body, jax.ShapeDtypeStruct((1, ROW_DEV), F32), 1 << 20, 1 << 16, name="pick"
    )(label, slot, returned)
    return picked.reshape(ROW_DEV)


def solution(mesh):
    fine = Mesh(mesh.devices.reshape(SIZES), AXES)
    return jax.shard_map(
        per_device,
        mesh=fine,
        in_specs=(P(AXES, None), P(AXES, None)),
        out_specs=P(AXES),
        check_vma=False,
    )
```

```python
import math

import jax
import jax.numpy as jnp
from jax import lax
from jax.experimental import pallas as pl
from jax.experimental.pallas import tpu as pltpu
from jax.sharding import Mesh, PartitionSpec as P

ITERS = 2
EPS = 1e-06
RIDGE = 0.001

AXES = ("y", "xh", "xl", "z", "c")
SIZES = (8, 2, 2, 16, 2)
FINE = ("xl", "z", "c")
FLAT = ("y", "xh", "xl")
PLANE = ("c",) + FLAT

D = 512
ROW_DEV = 512
ROWS = 524288
N_FINE = 64
N_PLANE = 64
N_Z = 16
CAP = 16
SLOTS = N_FINE * CAP
BLOCK = 128
BLOCKS = D // BLOCK
HALF = D // 2
PARTS = 2

STRIP = 3 * BLOCK
STRIP_ROWS = D // N_PLANE
SHRINK = 2.0 ** -12
CHIP_SHRINK = 2.0 ** -7
DOUBLING = (
    (("y",), 4, 16),
    (("y",), 2, 8),
    (("y",), 1, 4),
    (("xh", "xl"), 3, 3),
    (("xl",), 1, 1),
)

F32 = jnp.float32
BF16 = jnp.bfloat16
F16 = jnp.float16


def iota(shape, dim):
    return lax.broadcasted_iota(jnp.int32, shape, dim)


VMEM = pl.BlockSpec(memory_space=pltpu.VMEM)
SMEM = pl.BlockSpec(memory_space=pltpu.SMEM)


def call(body, outs, flops, moved, scratch=(), name=None, specs=None, room=48):
    return pl.pallas_call(
        body,
        **({} if specs is None else dict(in_specs=specs)),
        out_shape=outs,
        scratch_shapes=scratch,
        name=name,
        compiler_params=pltpu.CompilerParams(vmem_limit_bytes=room << 20),
        cost_estimate=pl.CostEstimate(flops=flops, bytes_accessed=moved, transcendentals=0),
    )


def gram_body(rows_ref, out_ref, held_ref, sems):
    part = ROW_DEV // PARTS
    copies = [
        pltpu.make_async_copy(
            rows_ref.at[pl.ds(i * part, part), :], held_ref.at[pl.ds(i * part, part), :], sems.at[i]
        )
        for i in range(PARTS)
    ]
    for copy in copies:
        copy.start()
    gram = None
    for i, copy in enumerate(copies):
        copy.wait()
        rows = held_ref[i * part:(i + 1) * part, :]
        term = lax.dot_general(rows, rows, (((0,), (0,)), ((), ())), preferred_element_type=F32)
        gram = term if gram is None else gram + term
    for b in range(BLOCKS):
        for k in range(3):
            c = (b + k) % BLOCKS
            out_ref[b * BLOCK:(b + 1) * BLOCK, k * BLOCK:(k + 1) * BLOCK] = gram[
                b * BLOCK:(b + 1) * BLOCK, c * BLOCK:(c + 1) * BLOCK
            ].astype(out_ref.dtype)


def pack_body(label_ref, rows_ref, out_ref, slot_ref):
    label = label_ref[...]
    onehot = (iota((N_FINE, ROW_DEV), 0) == label).astype(F32)
    earlier = (iota((ROW_DEV, ROW_DEV), 0) < iota((ROW_DEV, ROW_DEV), 1)).astype(BF16)
    rank = jnp.dot(onehot.astype(BF16), earlier, preferred_element_type=F32)
    slot = jnp.sum(onehot * rank, axis=0, keepdims=True).astype(jnp.int32)
    slot_ref[...] = slot
    place = label * CAP + slot
    chosen = (iota((SLOTS, ROW_DEV), 0) == place).astype(F32).astype(BF16)
    packed = jnp.dot(chosen, rows_ref[...], preferred_element_type=F32)
    filled = jnp.dot(chosen, jnp.ones((ROW_DEV, BLOCK), BF16), preferred_element_type=F32) > 0.5
    for k in range(D // BLOCK):
        part = packed[:, k * BLOCK:(k + 1) * BLOCK]
        out_ref[:, k * BLOCK:(k + 1) * BLOCK] = jnp.where(filled, part, jnp.nan).astype(BF16)


def parts_of(value):
    upper = value.astype(BF16)
    return upper, (value - upper.astype(F32)).astype(BF16)


def product(left, right):
    def dot(a, b):
        return jnp.dot(a, b, preferred_element_type=F32)

    return dot(left[0], right[0]) + (dot(left[0], right[1]) + dot(left[1], right[0]))


def root_body(me_ref, both_ref, out_ref, strip_ref, full_ref):
    half = N_PLANE // 2
    for k in range(N_PLANE):
        differs = 0
        for bit, (_, _, mask) in enumerate(DOUBLING):
            if k >> bit & 1:
                differs ^= mask
        to = (me_ref[0] ^ differs) + k // half * half
        to = pl.multiple_of(to * STRIP_ROWS, STRIP_ROWS)
        strip_ref[pl.ds(to, STRIP_ROWS), :] = both_ref[k * STRIP_ROWS:(k + 1) * STRIP_ROWS, :]
    for b in range(BLOCKS):
        for k in range(BLOCKS):
            c = (b + k) % BLOCKS
            if k < 3:
                piece = strip_ref[b * BLOCK:(b + 1) * BLOCK, k * BLOCK:(k + 1) * BLOCK]
            else:
                piece = strip_ref[c * BLOCK:(c + 1) * BLOCK, BLOCK:2 * BLOCK].T
            full_ref[b * BLOCK:(b + 1) * BLOCK, c * BLOCK:(c + 1) * BLOCK] = piece
    identity = (iota((D, D), 0) == iota((D, D), 1)).astype(F32)
    second = full_ref[...] / ROWS + RIDGE * identity
    norm_scale = jnp.max(jnp.sum(jnp.abs(second), axis=0, keepdims=True), axis=1, keepdims=True)
    root_est = second / norm_scale
    inverse_est = 0.5 * (3.0 * identity - root_est)
    first = parts_of(inverse_est)
    root_est = product(parts_of(root_est), first)
    newton_step = 0.5 * (3.0 * identity - product(first, parts_of(root_est)))
    inverse_est = product(parts_of(newton_step), first)
    out_ref[...] = (inverse_est / jnp.sqrt(norm_scale)).astype(BF16)


def best_body(rows_ref, whiten_ref, out_ref):
    rows = rows_ref[...].astype(F32)
    present = rows == rows
    clean = jnp.where(present, rows, 0.0).astype(BF16)
    whitened = jnp.dot(clean, whiten_ref[...], preferred_element_type=F32)
    meansq = jnp.mean(whitened * whitened, axis=-1, keepdims=True)
    unit = (whitened * lax.rsqrt(D * (meansq + EPS))).astype(BF16)
    bias = jnp.where(present[:, :1], 0.0, -4.0)
    tile = 256
    own = iota((tile, tile), 0) == iota((tile, tile), 1)
    columns = []
    for c in range(SLOTS // tile):
        best = jnp.full((1, tile), -1.0, F32)
        for b in range(SLOTS // tile):
            similar = lax.dot_general(
                unit[b * tile:(b + 1) * tile], unit[c * tile:(c + 1) * tile],
                (((1,), (1,)), ((), ())), preferred_element_type=F32,
            ) + bias[b * tile:(b + 1) * tile]
            if b == c:
                similar = jnp.where(own, -1.0, similar)
            best = jnp.maximum(best, jnp.max(similar, axis=0, keepdims=True))
        columns.append(best)
    best = jnp.concatenate(columns, axis=1)
    for source in range(N_FINE):
        out_ref[source:source + 1, :] = best[:, source * CAP:(source + 1) * CAP]


def pick_body(label_ref, slot_ref, best_ref, out_ref):
    onehot = (iota((N_FINE, ROW_DEV), 0) == label_ref[...]).astype(F32)
    mine = lax.dot_general(
        best_ref[...], onehot, (((0,), (0,)), ((), ())),
        precision=lax.Precision.HIGHEST, preferred_element_type=F32,
    )
    chosen = iota((CAP, ROW_DEV), 0) == slot_ref[...]
    out_ref[...] = jnp.sum(jnp.where(chosen, mine, 0.0), axis=0, keepdims=True)


def swap(value, axes):
    return lax.all_to_all(value, axes, split_axis=0, concat_axis=0, tiled=True)


def per_device(embeddings, labels):
    label = labels.reshape(1, ROW_DEV)
    strips = call(
        gram_body, jax.ShapeDtypeStruct((D, STRIP), BF16), 2 * ROW_DEV * D * D, 1 << 20,
        (pltpu.VMEM((ROW_DEV, D), BF16), pltpu.SemaphoreType.DMA((PARTS,))), name="gram",
        specs=(pl.BlockSpec(memory_space=pltpu.HBM),),
    )(pltpu.with_memory_space_constraint(embeddings, pltpu.HBM))
    both = lax.all_gather(strips, "c", axis=0, tiled=True)
    at = lax.axis_index("c") * HALF
    strips = sum(
        lax.dynamic_slice(
            both, (start, 0), (HALF, STRIP), allow_negative_indices=False
        ).astype(F32)
        for start in (at, at + D)
    )
    strips = (strips * CHIP_SHRINK).astype(F16)
    parts = swap(strips.reshape(N_PLANE // 2, STRIP_ROWS, STRIP), FLAT)

    outgoing, slot = call(
        pack_body,
        (
            jax.ShapeDtypeStruct((SLOTS, D), BF16),
            jax.ShapeDtypeStruct((1, ROW_DEV), jnp.int32),
        ),
        2 * SLOTS * ROW_DEV * D, 2 << 20, name="pack",
    )(label, embeddings)
    received = swap(outgoing.reshape(N_FINE, CAP, D), FINE).reshape(SLOTS, D)

    strip = (jnp.sum(parts.astype(F32), axis=0) * (SHRINK / CHIP_SHRINK)).astype(F16)
    layers = swap(jnp.broadcast_to(strip, (N_Z, STRIP_ROWS, STRIP)), "z")
    strip = jnp.sum(layers.astype(F32), axis=0) * (1.0 / SHRINK)
    for axes, differs, _ in DOUBLING:
        size = math.prod(SIZES[AXES.index(axis)] for axis in axes)
        other = lax.ppermute(strip, axes, [(i, i ^ differs) for i in range(size)])
        strip = jnp.concatenate([strip, other], axis=0)
    both = lax.all_gather(strip, "c", axis=0, tiled=True)
    whiten_b = call(
        root_body, jax.ShapeDtypeStruct((D, D), BF16), 18 * D * D * D, 2 << 20,
        (pltpu.VMEM((D, STRIP), F32), pltpu.VMEM((D, D), F32)), name="root",
        specs=(SMEM, VMEM),
    )(lax.axis_index(FLAT).reshape(1), both)

    best = call(
        best_body, jax.ShapeDtypeStruct((N_FINE, CAP), F32),
        2 * SLOTS * D * (D + SLOTS), 2 << 20, name="best",
    )(received, whiten_b)
    returned = swap(best.reshape(N_FINE, 1, CAP), FINE).reshape(N_FINE, CAP)
    picked = call(
        pick_body, jax.ShapeDtypeStruct((1, ROW_DEV), F32), 1 << 20, 1 << 16, name="pick"
    )(label, slot, returned)
    return picked.reshape(ROW_DEV)


def solution(mesh):
    fine = Mesh(mesh.devices.reshape(SIZES), AXES)
    return jax.shard_map(
        per_device,
        mesh=fine,
        in_specs=(P(AXES, None), P(AXES, None)),
        out_specs=P(AXES),
        check_vma=False,
    )
```
